128 devices in a mesh: ctx: 32 (over x, z, core), head: 4 (over y).
Axes of the slice: x: 4, y: 4, z: 4, core: 2. Of those that a mesh axis runs over, the one named last changes fastest.
Arguments:
- queries: bfloat16 [32768, 4096], P('ctx', 'head'), may hold values from -104 to 104
- cache_keys: bfloat16 [12288, 4096], P('ctx', 'head'), may hold values from -4 to 4
- cache_values: bfloat16 [12288, 4096], P('ctx', 'head'), may hold values from -6 to 6
- reflect: bfloat16 [32, 32, 64, 128], P('ctx', 'head'), may hold values from -6 to 6
- betas: bfloat16 [32, 32, 64], P('ctx', 'head'), may hold values from 0.099609375 to 1.8984375
- chain_len: int32 [32], P('ctx'), may hold values from 4 to 9, as said below
- block_start: int32 [32, 4], P('ctx'), may hold values from 0 to 128
- live_len: int32 [32], P('ctx'), may hold values from 1 to 384
- w_out: bfloat16 [4096, 4096], P('head'), may hold values from -0.75 to 0.75
Outputs:
- projected: bfloat16 [32768, 4096], P('ctx', 'head')
The draws below stay inside these ranges and needn't reach their ends.
Inputs may be any that keep to these rules, and one draw needn't show every extreme that they name: `chain_len`: every draw holds a request with 9 shards and one with 4.
All inputs are finite; a program needn't handle non-finite values.
Results may differ from the reference program's by a relative error of at most 0.012.
Values may be sent and summed in bfloat16 or wider, within the bound.
No kernel may reach another device: no remote copies, remote signals or barrier semaphores. Data moves between devices by JAX's collectives and lax.ppermute only.
A program may use at most 128 MiB of HBM per device.

```python
import jax
import jax.numpy as jnp
from jax import lax

D = 4096
H = 32
DH = 128
SHARD = 384
QB = 256
NQB = 4
RANK = 64
CHAIN = 9
ROWS = 32768
KEYS = 12288
N_CTX = 32
N_HEAD = 4


def key_table(key):
    samples = jax.random.truncated_normal(jax.random.fold_in(key, 101), -4.0, 4.0, (KEYS, D), jnp.float32)
    return samples


def draw_cache_keys(key, part):
    return key_table(key).astype(jnp.bfloat16)


def draw_queries(key, part):
    samples = 1.5 * jax.random.truncated_normal(jax.random.fold_in(key, 202), -4.0, 4.0, (ROWS, D), jnp.float32)
    return samples.astype(jnp.bfloat16)


def draw_chain_len(key, part):
    levels = jax.random.randint(jax.random.fold_in(key, 404), (N_CTX,), 0, 6)
    lengths = jnp.minimum(4 + levels * levels // 5, CHAIN)
    longest = jax.random.randint(jax.random.fold_in(key, 505), (), 0, N_CTX)
    offset = jax.random.randint(jax.random.fold_in(key, 606), (), 1, N_CTX)
    lengths = lengths.at[longest].set(CHAIN)
    lengths = lengths.at[(longest + offset) % N_CTX].set(4)
    return lengths.astype(jnp.int32)


def plant(values, rng, smallest, high):
    place = [jax.random.randint(jax.random.fold_in(rng, axis), (), 0, length) for axis, length in enumerate(values.shape)]
    main_axis = values.shape.index(max(values.shape))
    neighbour = place[:main_axis] + [(place[main_axis] + 1) % values.shape[main_axis]] + place[main_axis + 1:]
    return values.at[tuple(place)].set(smallest).at[tuple(neighbour)].set(high)


def block_levels(rng, extent, cuts, low, high):
    loudness, own = 1.0, jax.random.fold_in(rng, 6)
    for position, parts in cuts:
        heights = jnp.exp(jax.random.uniform(jax.random.fold_in(own, position), (parts,), jnp.float32, low / len(cuts), high / len(cuts)))
        loudness = loudness * jnp.repeat(heights, extent[position] // parts).reshape([-1 if axis == position else 1 for axis in range(len(extent))])
    return loudness


def normal_values(key, shape, scale, reach, split=(), held_as=jnp.bfloat16):
    drawn = scale * jax.random.normal(key, shape, jnp.float32)
    if split:
        drawn = drawn * block_levels(key, shape, split, -0.22, 0.18)
    return jnp.clip(drawn, -reach, reach).astype(held_as)


def setup_inputs(seed: int = 0) -> dict:
    seeds = jax.random.split(jax.random.key(seed), 10)
    return {
        "queries": draw_queries(jax.random.fold_in(seeds[9], 71), 0),
        "cache_keys": draw_cache_keys(jax.random.fold_in(seeds[9], 71), 0),
        "cache_values": normal_values(seeds[2], (KEYS, D), 1.0, 6.0, ((0, 32), (1, 4))),
        "reflect": normal_values(seeds[3], (N_CTX, H, RANK, DH), 1.0, 6.0, ((0, 32), (1, 4))),
        "betas": jnp.clip(0.099609375 + 1.7988281 * jax.random.uniform(seeds[4], (N_CTX, H, RANK), jnp.float32) ** block_levels(seeds[4], (N_CTX, H, RANK), ((0, 32), (1, 4)), -0.2, 0.2), 0.099609375, 1.8984375).astype(jnp.bfloat16),
        "chain_len": draw_chain_len(jax.random.fold_in(seeds[9], 71), 0),
        "block_start": plant(jax.random.randint(seeds[6], (N_CTX, NQB), 0, SHARD - QB + 1), jax.random.fold_in(seeds[6], 1), 0, SHARD - QB).astype(jnp.int32),
        "live_len": plant(jax.random.randint(seeds[7], (N_CTX,), 1, SHARD + 1), jax.random.fold_in(seeds[7], 1), 1, SHARD).astype(jnp.int32),
        "w_out": normal_values(seeds[8], (D, D), (D // 64) ** -0.5, 0.75, ((0, 4),)),
    }


def rounded(tensor):
    return lax.optimization_barrier(tensor.astype(jnp.bfloat16)).astype(jnp.float32)

def shard_products(reflect, betas):
    unit_rows = reflect.astype(jnp.float32)
    unit_rows = unit_rows / jnp.sqrt(lax.optimization_barrier(jnp.sum(unit_rows * unit_rows, axis=-1, keepdims=True)) + 1e-06)
    rates = betas.astype(jnp.float32)
    initial = jnp.broadcast_to(jnp.eye(DH, dtype=jnp.float32), (N_CTX, H, DH, DH))

    def reflect_once(product, column):
        vector = lax.dynamic_index_in_dim(unit_rows, column, 2, keepdims=False)
        weight = lax.dynamic_index_in_dim(rates, column, 2, keepdims=False)
        applied = jnp.einsum('shij,shj->shi', product, vector, precision=lax.Precision.HIGHEST)
        return (product - weight[:, :, None, None] * applied[:, :, :, None] * vector[:, :, None, :], None)
    product, unused = lax.scan(reflect_once, initial, jnp.arange(RANK))
    return product

def reference(queries, cache_keys, cache_values, reflect, betas, chain_len, block_start, live_len, w_out):
    products = shard_products(reflect, betas)
    key_layout = cache_keys.reshape(N_CTX, SHARD, H, DH)
    value_layout = cache_values.reshape(N_CTX, SHARD, H, DH)
    query_layout = queries.reshape(N_CTX, NQB * QB, H, DH)
    request_rows = NQB * QB
    scale = DH ** (-0.5)
    key_index = jnp.arange(SHARD)
    group_width = D // N_HEAD

    def one_request(request):
        carried = lax.dynamic_index_in_dim(query_layout, request, 0, keepdims=False).astype(jnp.float32)
        positions = (block_start[request][:, None] + jnp.arange(QB)[None, :]).reshape(request_rows)
        length = chain_len[request]
        live_count = live_len[request]
        initial = (carried, jnp.full((H, request_rows), -jnp.inf, jnp.float32), jnp.zeros((H, request_rows), jnp.float32), jnp.zeros((request_rows, H, DH), jnp.float32))

        def visit(carry, distance):
            carried, row_top, row_total, summed = carry
            shard_id = (request - distance) % N_CTX
            shard_keys = lax.dynamic_index_in_dim(key_layout, shard_id, 0, keepdims=False).astype(jnp.float32)
            shard_values = lax.dynamic_index_in_dim(value_layout, shard_id, 0, keepdims=False).astype(jnp.float32)
            active = distance < length
            allowed = jnp.where(distance == 0, key_index[None, :] <= positions[:, None], jnp.where(distance == length - 1, key_index[None, :] >= SHARD - live_count, True))
            allowed = allowed & active
            scores = jnp.einsum('rhd,khd->hrk', rounded(carried), shard_keys) * scale
            scores = jnp.where(allowed[None], scores, -jnp.inf)
            block_top = lax.optimization_barrier(jnp.max(scores, axis=-1))
            safe_top = jnp.where(active, block_top, 0.0)
            weights = rounded(jnp.exp(scores - safe_top[..., None]))
            block_total = lax.optimization_barrier(jnp.sum(weights, axis=-1))
            block_sum = jnp.einsum('hrk,khd->rhd', weights, shard_values)
            new_top = jnp.where(active, jnp.maximum(row_top, block_top), row_top)
            old_factor = jnp.exp(row_top - new_top)
            new_factor = jnp.where(active, jnp.exp(block_top - new_top), 0.0)
            row_total = row_total * old_factor + new_factor * block_total
            summed = summed * old_factor.T[:, :, None] + new_factor.T[:, :, None] * block_sum
            product = lax.dynamic_index_in_dim(products, shard_id, 0, keepdims=False)
            carried = jnp.einsum('rhd,hde->rhe', carried, product, precision=lax.Precision.HIGHEST)
            return ((carried, new_top, row_total, summed), None)
        finished, unused = lax.scan(visit, initial, jnp.arange(CHAIN))
        attended = rounded((finished[3] / finished[2].T[:, :, None]).reshape(request_rows, D))
        outcome = jnp.zeros((request_rows, D), jnp.float32)
        for group in range(N_HEAD):
            columns = attended[:, group * group_width:(group + 1) * group_width]
            weight_rows = w_out[group * group_width:(group + 1) * group_width].astype(jnp.float32)
            outcome = outcome + rounded(jnp.dot(columns, weight_rows, preferred_element_type=jnp.float32))
        return outcome.astype(jnp.bfloat16)
    projected = lax.map(one_request, jnp.arange(N_CTX))
    return projected.reshape(ROWS, D)
```

```python
import functools

import jax
import jax.numpy as jnp
import numpy as np
from jax import lax
from jax.experimental import pallas as pl
from jax.experimental.pallas import tpu as pltpu
from jax.sharding import PartitionSpec as P

N_CTX = 32
N_HEAD = 4
HEADS = 8
HALF = 4
DH = 128
SHARD = 384
ROWS = 1024
QB = 256
NQB = 4
RANK = 64
CHAIN = 9
NEIGH = 5
PRE = 0.125
LOG2E = 1.4426950408889634
POST = float(DH ** (-0.5) * LOG2E / PRE)
bf16 = jnp.bfloat16
f32 = jnp.float32


SWAP = [(s, s ^ 1) for s in range(N_CTX)]


def plane(step):
    return [(s, (s + 8 * step) % N_CTX) for s in range(N_CTX)]


def chips(step):
    return [(s, (s + 2 * step) % N_CTX) for s in range(N_CTX)]


def along_z(step):
    return [(s, (s // 8) * 8 + (s + 2 * step) % 8) for s in range(N_CTX)]


def along_y(step):
    return [(s, (s + step) % N_HEAD) for s in range(N_HEAD)]


def split(value):
    high = value.astype(bf16)
    low = (value - high.astype(f32)).astype(bf16)
    return high, low


def dot3(left, right, dims):
    def dot(a, b):
        return lax.dot_general(a, b, (dims, ((), ())), preferred_element_type=f32)

    left_high, left_low = split(left)
    right_high, right_low = split(right)
    return dot(left_high, right_high) + (dot(left_high, right_low) + dot(left_low, right_high))


def pack_kernel(core_ref, km, kt, vm, vt, qm, qt, kv_mine, kv_theirs, q_mine, q_theirs):
    for key, value, out in ((km, vm, kv_mine), (kt, vt, kv_theirs)):
        for part in range(3):
            rows = pl.ds(part * DH, DH)
            out[0, 0, part] = key[rows, :]
            out[0, 1, part] = value[rows, :].T
    q_mine[0] = qm[...]
    q_theirs[0] = qt[...]


def pack(core, keys, values, queries):
    def mine(h, c):
        return (0, HALF * c[0] + h)

    def theirs(h, c):
        return (0, HALF * (1 - c[0]) + h)

    kv_out = pl.BlockSpec((1, 2, 3, DH, DH), lambda h, c: (h, 0, 0, 0, 0))
    q_out = pl.BlockSpec((1, ROWS, DH), lambda h, c: (h, 0, 0))
    in_specs = []
    for rows in (SHARD, SHARD, ROWS):
        in_specs += [pl.BlockSpec((rows, DH), mine), pl.BlockSpec((rows, DH), theirs)]
    kv_shape = jax.ShapeDtypeStruct((HALF, 2, 3, DH, DH), bf16)
    q_shape = jax.ShapeDtypeStruct((HALF, ROWS, DH), bf16)
    return pl.pallas_call(
        pack_kernel,
        out_shape=(kv_shape, kv_shape, q_shape, q_shape),
        grid_spec=pltpu.PrefetchScalarGridSpec(
            num_scalar_prefetch=1,
            grid=(HALF,),
            in_specs=in_specs,
            out_specs=(kv_out, kv_out, q_out, q_out),
        ),
        name="pack",
    )(core, keys, keys, values, values, queries, queries)


def turns_kernel(core_ref, r0, r1, r2, r3, r4, out):
    core = core_ref[0]
    sources = (r0, r1, r2, r3, r4)
    row = lax.broadcasted_iota(jnp.int32, (RANK, RANK), 0)
    col = lax.broadcasted_iota(jnp.int32, (RANK, RANK), 1)
    big_row = lax.broadcasted_iota(jnp.int32, (DH, DH), 0)
    big_col = lax.broadcasted_iota(jnp.int32, (DH, DH), 1)
    eye = jnp.where(big_row == big_col, 1.0, 0.0).astype(f32)
    backs = []
    for item in range(CHAIN):
        parity = 1 - item % 2
        slot = parity ^ core
        data = sources[item // 2][slot, 0].astype(f32)
        rows = data[:RANK]
        unit = rows / jnp.sqrt(jnp.sum(rows * rows, axis=-1, keepdims=True) + 1e-06)
        rates = data[RANK : RANK + 1, :RANK]
        rate = jnp.sum(jnp.where(row == col, rates, 0.0), axis=1, keepdims=True)
        gram = dot3(unit, unit, ((1,), (1,)))
        lower = rate * jnp.where(row > col, gram, 0.0)
        scaled = rate * unit
        pieces = [scaled[8 * i : 8 * i + 8] for i in range(RANK // 8)]
        for j in range(RANK - 1):
            here = pieces[j // 8][j % 8 : j % 8 + 1]
            for i in range(j // 8, RANK // 8):
                if i == j // 8 and j % 8 == 7:
                    continue
                pieces[i] = pieces[i] - lower[8 * i : 8 * i + 8, j : j + 1] * here
        solved = jnp.concatenate(pieces, axis=0)
        backs.append(eye - dot3(unit, solved, ((0,), (0,))))
    for parity in range(2):
        total = backs[1 - parity]
        for m in range(1, CHAIN):
            if m > 1:
                total = dot3(backs[m - parity], total, ((1,), (0,)))
            high, low = split(total * (PRE * POST))
            out[parity ^ core, 0, m - 1, :DH, :] = high
            out[parity ^ core, 0, m - 1, DH:, :] = low


def turns(core, factors):
    spec = pl.BlockSpec((2, 1, 80, DH), lambda h, c: (0, h, 0, 0))
    return pl.pallas_call(
        turns_kernel,
        out_shape=jax.ShapeDtypeStruct((2, HALF, CHAIN - 1, 2 * DH, DH), bf16),
        grid_spec=pltpu.PrefetchScalarGridSpec(
            num_scalar_prefetch=1,
            grid=(HALF,),
            in_specs=[spec] * NEIGH,
            out_specs=pl.BlockSpec(
                (2, 1, CHAIN - 1, 2 * DH, DH), lambda h, c: (0, h, 0, 0, 0)
            ),
        ),
        name="turns",
    )(core, *factors)


def attend_kernel(
    info, qm, qt, turn, kv0, kv1, kv2, kv3, kv4, out, keys, vals, q_cols, top, acc
):
    request = pl.program_id(0)
    core = info[0]
    parity = core ^ request
    base = 1 + 8 * request
    length = info[base]
    live = info[base + 1]

    @pl.when(request == 0)
    def _():
        q_cols[...] = qm[0].T

    @pl.when(request == 1)
    def _():
        q_cols[...] = qt[0].T

    for near, source in enumerate((kv0, kv1, kv2, kv3, kv4)):
        for slot in range(2):
            step = 2 * near - (slot ^ core) + parity

            @pl.when((step >= 0) & (step < length))
            def _():
                block = source[slot, 0].reshape(SHARD, DH)
                for part in range(3):
                    vals[step, :DH, part * DH : (part + 1) * DH] = source[slot, 1, part]
                vals[step, DH:, :] = jnp.ones((16, SHARD), bf16)

                @pl.when(step == 0)
                def _():
                    keys[0] = (block.astype(f32) * PRE).astype(bf16)

                @pl.when(step > 0)
                def _():
                    doubled = jnp.concatenate([block, block], axis=1)
                    keys[step] = jnp.dot(
                        doubled, turn[0, 0, step - 1], preferred_element_type=f32
                    ).astype(bf16)

    key_index = lax.broadcasted_iota(jnp.int32, (SHARD, QB), 0)
    lane = lax.broadcasted_iota(jnp.int32, (1, QB), 1)

    for tile in range(NQB):
        columns = pl.ds(tile * QB, QB)
        scores = jnp.dot(keys[0], q_cols[:, columns], preferred_element_type=f32) * POST
        position = info[base + 2 + tile] + lane
        scores = jnp.where(key_index <= position, scores, -jnp.inf)
        high = jnp.max(scores, axis=0, keepdims=True)
        weights = jnp.exp2(scores - high).astype(bf16)
        top[:, columns] = high
        acc[tile] = jnp.dot(vals[0], weights, preferred_element_type=f32)

    def visit(step, masked):
        for tile in range(NQB):
            columns = pl.ds(tile * QB, QB)
            scores = jnp.dot(keys[step], q_cols[:, columns], preferred_element_type=f32)
            if masked:
                scores = jnp.where(key_index >= SHARD - live, scores, -jnp.inf)
            before = top[:, columns]
            high = jnp.maximum(before, jnp.max(scores, axis=0, keepdims=True))
            weights = jnp.exp2(scores - high).astype(bf16)
            top[:, columns] = high
            acc[tile] = acc[tile] * jnp.exp2(before - high) + jnp.dot(
                vals[step], weights, preferred_element_type=f32
            )

    def inner(step, carry):
        visit(step, False)
        return carry

    lax.fori_loop(1, length - 1, inner, 0)
    visit(length - 1, True)
    for tile in range(NQB):
        done = acc[tile, :DH] / acc[tile, DH : DH + 1]
        out[0, tile * QB : (tile + 1) * QB, :] = done.T.astype(bf16)


def attend(head, info, q_mine, q_theirs, turn, blocks):
    whole = pl.BlockSpec((2, 2, 3, DH, DH), lambda r, c: (0, 0, 0, 0, 0))
    q_spec = pl.BlockSpec((1, ROWS, DH), lambda r, c: (head, 0, 0))
    return pl.pallas_call(
        attend_kernel,
        out_shape=jax.ShapeDtypeStruct((2, ROWS, DH), bf16),
        grid_spec=pltpu.PrefetchScalarGridSpec(
            num_scalar_prefetch=1,
            grid=(2,),
            in_specs=[
                q_spec,
                q_spec,
                pl.BlockSpec(
                    (1, 1, CHAIN - 1, 2 * DH, DH), lambda r, c: (r, head, 0, 0, 0)
                ),
            ]
            + [whole] * NEIGH,
            out_specs=pl.BlockSpec((1, ROWS, DH), lambda r, c: (r, 0, 0)),
            scratch_shapes=[
                pltpu.VMEM((CHAIN, SHARD, DH), bf16),
                pltpu.VMEM((CHAIN, DH + 16, SHARD), bf16),
                pltpu.VMEM((DH, ROWS), bf16),
                pltpu.VMEM((1, ROWS), f32),
                pltpu.VMEM((NQB, DH + 16, QB), f32),
            ],
        ),
        name=f"attend{head}",
    )(info, q_mine, q_theirs, turn, *blocks)


def project_kernel(count, last, *refs):
    inputs = 4 * (count + 2)
    atts = refs[: 4 * count]
    weights = refs[4 * count : inputs]
    rest = refs[inputs:]
    total = rest[0][...] if last else None
    for source in range(4):
        for slot in range(2):
            rows = jnp.concatenate(
                [atts[source * count + h][slot] for h in range(count)], axis=1
            )
            matrix = weights[2 * source + slot][...].reshape(count * DH, -1)
            part = jnp.dot(rows, matrix, preferred_element_type=f32)
            total = part if total is None else total + part
    rest[-1][...] = total.astype(rest[-1].dtype)


def project(atts, weights, first, total, dtype):
    count = len(atts[0])
    flat = [array for source in atts for array in source]
    flat_weights = [array for source in weights for array in source]
    att_spec = pl.BlockSpec((2, QB, DH), lambda r: (0, r, 0))
    weight_spec = pl.BlockSpec((count, DH, ROWS), lambda r: (first // count, 0, 0))
    total_spec = pl.BlockSpec((QB, ROWS), lambda r: (r, 0))
    return pl.pallas_call(
        functools.partial(project_kernel, count, total is not None),
        out_shape=jax.ShapeDtypeStruct((ROWS, ROWS), dtype),
        grid=(ROWS // QB,),
        in_specs=[att_spec] * len(flat)
        + [weight_spec] * len(flat_weights)
        + ([total_spec] if total is not None else []),
        out_specs=total_spec,
        name=f"project{first}",
    )(*flat, *flat_weights, *(() if total is None else (total,)))


def shards(
    queries, cache_keys, cache_values, reflect, betas, chain_len, block_start, live_len, w_out
):
    here = lax.axis_index("ctx")
    group = lax.axis_index("head")
    core = here % 2
    z = (here % 8) // 2
    core_array = core[None].astype(jnp.int32)

    own_info = jnp.concatenate(
        [chain_len, live_len, block_start[0], jnp.zeros((2,), jnp.int32)]
    )
    info = jnp.concatenate([core_array, own_info, lax.ppermute(own_info, "ctx", SWAP)])

    rates = jnp.pad(betas[0][:, None, :], ((0, 0), (0, 15), (0, DH - RANK)))
    factors = jnp.concatenate([reflect[0], rates], axis=1)
    factors_mine = lax.dynamic_slice_in_dim(factors, HALF * core, HALF, 0)
    factors_theirs = lax.dynamic_slice_in_dim(factors, HALF * (1 - core), HALF, 0)
    factors_pair = jnp.stack([factors_mine, lax.ppermute(factors_theirs, "ctx", SWAP)])
    factor_list = [factors_pair] + [
        lax.ppermute(factors_pair, "ctx", chips(step)) for step in range(1, NEIGH)
    ]

    kv_mine, kv_theirs, q_mine, q_theirs = pack(core_array, cache_keys, cache_values, queries)
    kv_other = lax.ppermute(kv_theirs, "ctx", SWAP)
    q_other = lax.ppermute(q_theirs, "ctx", SWAP)

    pairs = [jnp.stack([kv_mine[h], kv_other[h]]) for h in range(HALF)]
    previous = [lax.ppermute(pair, "ctx", plane(1)) for pair in pairs]
    blocks = []
    for h in range(HALF):
        arrived = [
            lax.ppermute(
                jnp.where(z + step >= 4, previous[h], pairs[h]), "ctx", along_z(step)
            )
            for step in range(1, 4)
        ]
        blocks.append([pairs[h], *arrived, previous[h]])

    def columns_of(half, step):
        target = (group + step) % N_HEAD
        block = lax.dynamic_slice(
            w_out, (half * HALF * DH, target * ROWS), (HALF * DH, ROWS)
        )
        return block.reshape(HALF, DH, ROWS)

    weights = [(columns_of(core, 0), columns_of(1 - core, 0))]
    for step in range(1, N_HEAD):
        fetched = lax.ppermute(columns_of(core, step), "head", along_y(step))
        weights.append((fetched, lax.ppermute(fetched, "ctx", SWAP)))

    turn = turns(core_array, factor_list)
    atts = [[] for _ in range(N_HEAD)]
    for h in range(HALF):
        both = attend(h, info, q_mine, q_other, turn, blocks[h])
        rows = jnp.stack([both[0], lax.ppermute(both[1], "ctx", SWAP)])
        atts[0].append(rows)
        for step in range(1, N_HEAD):
            atts[step].append(lax.ppermute(rows, "head", along_y(step)))
    total = project([a[:2] for a in atts], weights, 0, None, f32)
    total = project([a[2:3] for a in atts], weights, 2, total, f32)
    return project([a[3:] for a in atts], weights, 3, total, bf16)


def solution(mesh):
    return jax.shard_map(
        shards,
        mesh=mesh,
        in_specs=(
            P("ctx", "head"),
            P("ctx", "head"),
            P("ctx", "head"),
            P("ctx", "head", None, None),
            P("ctx", "head", None),
            P("ctx"),
            P("ctx", None),
            P("ctx"),
            P("head", None),
        ),
        out_specs=P("ctx", "head"),
        check_vma=False,
    )
```

```python
import functools

import jax
import jax.numpy as jnp
from jax import lax
from jax.experimental import pallas as pl
from jax.experimental.pallas import tpu as pltpu
from jax.sharding import PartitionSpec as P

N_CTX = 32
N_HEAD = 4
HALF = 4
DH = 128
SHARD = 384
ROWS = 1024
QB = 256
NQB = 4
RANK = 64
CHAIN = 9
SUB = 16
BAND = 512
NEIGH = 5
PRE = 0.125
LOG2E = 1.4426950408889634
POST = float(DH ** (-0.5) * LOG2E / PRE)
bf16 = jnp.bfloat16
f32 = jnp.float32


SWAP = [(s, s ^ 1) for s in range(N_CTX)]


def plane(step):
    return [(s, (s + 8 * step) % N_CTX) for s in range(N_CTX)]


def chips(step):
    return [(s, (s + 2 * step) % N_CTX) for s in range(N_CTX)]


def along_z(step):
    return [(s, (s // 8) * 8 + (s + 2 * step) % 8) for s in range(N_CTX)]


def along_y(step):
    return [(s, (s + step) % N_HEAD) for s in range(N_HEAD)]


def split(value):
    high = value.astype(bf16)
    low = (value - high.astype(f32)).astype(bf16)
    return high, low


def dot3(left, right, dims):
    def dot(a, b):
        return lax.dot_general(a, b, (dims, ((), ())), preferred_element_type=f32)

    left_high, left_low = split(left)
    right_high, right_low = split(right)
    return dot(left_high, right_high) + (dot(left_high, right_low) + dot(left_low, right_high))


def pack_kernel(core_ref, km, kt, vm, vt, qm, qt, kv_mine, kv_theirs, q_mine, q_theirs):
    for key, value, out in ((km, vm, kv_mine), (kt, vt, kv_theirs)):
        for part in range(3):
            rows = pl.ds(part * DH, DH)
            out[0, 0, part] = key[rows, :]
            out[0, 1, part] = value[rows, :].T
    q_mine[0] = qm[...]
    q_theirs[0] = qt[...]


def pack(core, keys, values, queries):
    def mine(h, c):
        return (0, HALF * c[0] + h)

    def theirs(h, c):
        return (0, HALF * (1 - c[0]) + h)

    kv_out = pl.BlockSpec((1, 2, 3, DH, DH), lambda h, c: (h, 0, 0, 0, 0))
    q_out = pl.BlockSpec((1, ROWS, DH), lambda h, c: (h, 0, 0))
    in_specs = []
    for rows in (SHARD, SHARD, ROWS):
        in_specs += [pl.BlockSpec((rows, DH), mine), pl.BlockSpec((rows, DH), theirs)]
    kv_shape = jax.ShapeDtypeStruct((HALF, 2, 3, DH, DH), bf16)
    q_shape = jax.ShapeDtypeStruct((HALF, ROWS, DH), bf16)
    return pl.pallas_call(
        pack_kernel,
        out_shape=(kv_shape, kv_shape, q_shape, q_shape),
        grid_spec=pltpu.PrefetchScalarGridSpec(
            num_scalar_prefetch=1,
            grid=(HALF,),
            in_specs=in_specs,
            out_specs=(kv_out, kv_out, q_out, q_out),
        ),
        name="pack",
    )(core, keys, keys, values, values, queries, queries)


def turns_kernel(core_ref, r0, r1, r2, r3, r4, out):
    core = core_ref[0]
    sources = (r0, r1, r2, r3, r4)
    row = lax.broadcasted_iota(jnp.int32, (RANK, RANK), 0)
    col = lax.broadcasted_iota(jnp.int32, (RANK, RANK), 1)
    big_row = lax.broadcasted_iota(jnp.int32, (DH, DH), 0)
    big_col = lax.broadcasted_iota(jnp.int32, (DH, DH), 1)
    eye = jnp.where(big_row == big_col, 1.0, 0.0).astype(f32)
    backs = []
    for items in (range(CHAIN),):
        units, lowers, solving = [], [], []
        for item in items:
            slot = (1 - item % 2) ^ core
            data = sources[item // 2][slot, 0].astype(f32)
            rows = data[:RANK]
            unit = rows / jnp.sqrt(jnp.sum(rows * rows, axis=-1, keepdims=True) + 1e-06)
            rates = data[RANK : RANK + 1, :RANK]
            rate = jnp.sum(jnp.where(row == col, rates, 0.0), axis=1, keepdims=True)
            gram = dot3(unit, unit, ((1,), (1,)))
            units.append(unit)
            lowers.append(rate * jnp.where(row > col, gram, 0.0))
            scaled = rate * unit
            solving.append([scaled[SUB * i : SUB * i + SUB] for i in range(RANK // SUB)])
        for block in range(RANK // SUB):
            at = SUB * block
            for lower, pieces in zip(lowers, solving):
                upper, under = pieces[block][:8], pieces[block][8:]
                for j in range(SUB - 1):
                    here = upper[j : j + 1] if j < 8 else under[j - 8 : j - 7]
                    if j < 7:
                        upper = upper - lower[at : at + 8, at + j : at + j + 1] * here
                    under = under - lower[at + 8 : at + 16, at + j : at + j + 1] * here
                pieces[block] = jnp.concatenate([upper, under], axis=0)
            if block + 1 < RANK // SUB:
                for lower, pieces in zip(lowers, solving):
                    change = dot3(
                        lower[at + SUB :, at : at + SUB], pieces[block], ((1,), (0,))
                    )
                    for i in range(block + 1, RANK // SUB):
                        first = SUB * (i - block - 1)
                        pieces[i] = pieces[i] - change[first : first + SUB]
        for unit, pieces in zip(units, solving):
            solved = jnp.concatenate(pieces, axis=0)
            backs.append(eye - dot3(unit, solved, ((0,), (0,))))
    for parity in range(2):
        total = backs[1 - parity]
        for m in range(1, CHAIN):
            if m > 1:
                total = dot3(backs[m - parity], total, ((1,), (0,)))
            high, low = split(total * (PRE * POST))
            out[parity ^ core, 0, m - 1, :DH, :] = high
            out[parity ^ core, 0, m - 1, DH:, :] = low


def turns(core, factors):
    spec = pl.BlockSpec((2, 1, 80, DH), lambda h, c: (0, h, 0, 0))
    return pl.pallas_call(
        turns_kernel,
        out_shape=jax.ShapeDtypeStruct((2, HALF, CHAIN - 1, 2 * DH, DH), bf16),
        grid_spec=pltpu.PrefetchScalarGridSpec(
            num_scalar_prefetch=1,
            grid=(HALF,),
            in_specs=[spec] * NEIGH,
            out_specs=pl.BlockSpec(
                (2, 1, CHAIN - 1, 2 * DH, DH), lambda h, c: (0, h, 0, 0, 0)
            ),
        ),
        name="turns",
    )(core, *factors)


def attend_kernel(
    info, qm, qt, turn, kv0, kv1, kv2, kv3, kv4, out, keys, vals, q_cols, top, best,
    score, acc,
):
    request = pl.program_id(0)
    core = info[0]
    parity = core ^ request
    base = 1 + 8 * request
    length = info[base]
    live = info[base + 1]

    @pl.when(request == 0)
    def _():
        q_cols[...] = qm[0].T

    @pl.when(request == 1)
    def _():
        q_cols[...] = qt[0].T

    for near, source in enumerate((kv0, kv1, kv2, kv3, kv4)):
        for slot in range(2):
            step = 2 * near - (slot ^ core) + parity

            @pl.when((step >= 0) & (step < length))
            def _():
                block = source[slot, 0].reshape(SHARD, DH)
                for part in range(3):
                    vals[step, :DH, part * DH : (part + 1) * DH] = source[slot, 1, part]
                vals[step, DH:, :] = jnp.ones((16, SHARD), bf16)

                @pl.when(step == 0)
                def _():
                    keys[0] = (block.astype(f32) * PRE).astype(bf16)

                @pl.when(step > 0)
                def _():
                    doubled = jnp.concatenate([block, block], axis=1)
                    keys[step] = jnp.dot(
                        doubled, turn[0, 0, step - 1], preferred_element_type=f32
                    ).astype(bf16)

    key_index = lax.broadcasted_iota(jnp.int32, (DH, QB), 0)
    lane = lax.broadcasted_iota(jnp.int32, (1, QB), 1)

    def scored(step, tile, buffer, kind, part, high):
        rows = pl.ds(part * DH, DH)
        found = jnp.dot(
            keys[step, rows, :], q_cols[:, tile * QB : (tile + 1) * QB],
            preferred_element_type=f32,
        )
        if kind == "home":
            position = info[base + 2 + tile] + lane - part * DH
            found = jnp.where(key_index <= position, found * POST, -jnp.inf)
        elif kind == "oldest":
            found = jnp.where(key_index >= SHARD - live - part * DH, found, -jnp.inf)
        score[buffer, rows, :] = found
        best = jnp.max(found.reshape(DH // 8, 8, QB), axis=0)
        return best if high is None else jnp.maximum(high, best)

    def both(ahead, behind):
        high = None
        if behind is not None:
            step, tile, buffer, first = behind
            block = best[buffer]
            if first:
                limit = block
            else:
                before = top[tile]
                limit = jnp.maximum(before, block)
            parts = []
        for part in range(3):
            if ahead is not None:
                high = scored(*ahead, part, high)
            if behind is not None:
                rows = pl.ds(part * DH, DH)
                parts.append(jnp.exp2(score[buffer, rows, :] - limit).astype(bf16))
        if behind is not None:
            part = jnp.dot(
                vals[step], jnp.concatenate(parts, axis=0), preferred_element_type=f32
            )
            top[tile] = limit
            acc[tile] = part if first else acc[tile] * jnp.exp2(before - limit) + part
        if ahead is not None:
            best[ahead[2]] = jnp.max(high, axis=0, keepdims=True)

    order = [(0, tile, "home") for tile in range(NQB)]
    order += [(length - 1, tile, "oldest") for tile in range(NQB)]
    order += [(1, 0, "whole")]
    for at in range(len(order)):
        ahead = (order[at][0], order[at][1], at % 2, order[at][2])
        behind = None
        if at:
            behind = (order[at - 1][0], order[at - 1][1], (at - 1) % 2, at <= NQB)
        both(ahead, behind)

    def inner(step, carry):
        for tile in range(NQB):
            if tile + 1 < NQB:
                ahead = (step, tile + 1, (tile + 1) % 2, "whole")
            else:
                ahead = (jnp.minimum(step + 1, length - 2), 0, 0, "whole")
            both(ahead, (step, tile, tile % 2, False))
        return carry

    lax.fori_loop(1, length - 1, inner, 0)
    for tile in range(NQB):
        done = acc[tile, :DH] / acc[tile, DH : DH + 1]
        out[0, tile * QB : (tile + 1) * QB, :] = done.T.astype(bf16)


def attend(head, info, q_mine, q_theirs, turn, blocks):
    whole = pl.BlockSpec((2, 2, 3, DH, DH), lambda r, c: (0, 0, 0, 0, 0))
    q_spec = pl.BlockSpec((1, ROWS, DH), lambda r, c: (head, 0, 0))
    return pl.pallas_call(
        attend_kernel,
        out_shape=jax.ShapeDtypeStruct((2, ROWS, DH), bf16),
        grid_spec=pltpu.PrefetchScalarGridSpec(
            num_scalar_prefetch=1,
            grid=(2,),
            in_specs=[
                q_spec,
                q_spec,
                pl.BlockSpec(
                    (1, 1, CHAIN - 1, 2 * DH, DH), lambda r, c: (r, head, 0, 0, 0)
                ),
            ]
            + [whole] * NEIGH,
            out_specs=pl.BlockSpec((1, ROWS, DH), lambda r, c: (r, 0, 0)),
            scratch_shapes=[
                pltpu.VMEM((CHAIN, SHARD, DH), bf16),
                pltpu.VMEM((CHAIN, DH + 16, SHARD), bf16),
                pltpu.VMEM((DH, ROWS), bf16),
                pltpu.VMEM((NQB, 1, QB), f32),
                pltpu.VMEM((2, 1, QB), f32),
                pltpu.VMEM((2, SHARD, QB), f32),
                pltpu.VMEM((NQB, DH + 16, QB), f32),
            ],
        ),
    )(info, q_mine, q_theirs, turn, *blocks)


def project_kernel(count, last, *refs):
    inputs = 4 * (count + 2)
    atts = refs[: 4 * count]
    weights = refs[4 * count : inputs]
    rest = refs[inputs:]
    total = rest[0][...] if last else None
    for source in range(4):
        for slot in range(2):
            rows = jnp.concatenate(
                [atts[source * count + h][slot] for h in range(count)], axis=1
            )
            matrix = weights[2 * source + slot][...].reshape(count * DH, -1)
            part = jnp.dot(rows, matrix, preferred_element_type=f32)
            total = part if total is None else total + part
    rest[-1][...] = total.astype(rest[-1].dtype)


def project(atts, weights, first, total, dtype):
    count = len(atts[0])
    flat = [array for source in atts for array in source]
    flat_weights = [array for source in weights for array in source]
    att_spec = pl.BlockSpec((2, BAND, DH), lambda r: (0, r, 0))
    weight_spec = pl.BlockSpec((count, DH, ROWS), lambda r: (first // count, 0, 0))
    total_spec = pl.BlockSpec((BAND, ROWS), lambda r: (r, 0))
    return pl.pallas_call(
        functools.partial(project_kernel, count, total is not None),
        out_shape=jax.ShapeDtypeStruct((ROWS, ROWS), dtype),
        grid=(ROWS // BAND,),
        in_specs=[att_spec] * len(flat)
        + [weight_spec] * len(flat_weights)
        + ([total_spec] if total is not None else []),
        out_specs=total_spec,
    )(*flat, *flat_weights, *(() if total is None else (total,)))


def program(
    queries, cache_keys, cache_values, reflect, betas, chain_len, block_start, live_len, w_out
):
    here = lax.axis_index("ctx")
    group = lax.axis_index("head")
    core = here % 2
    z = (here % 8) // 2
    core_array = core[None].astype(jnp.int32)

    own_info = jnp.concatenate(
        [chain_len, live_len, block_start[0], jnp.zeros((2,), jnp.int32)]
    )
    info = jnp.concatenate([core_array, own_info, lax.ppermute(own_info, "ctx", SWAP)])

    kv_mine, kv_theirs, q_mine, q_theirs = pack(core_array, cache_keys, cache_values, queries)
    kv_other = lax.ppermute(kv_theirs, "ctx", SWAP)

    rates = jnp.pad(betas[0][:, None, :], ((0, 0), (0, 15), (0, DH - RANK)))
    factors = jnp.concatenate([reflect[0], rates], axis=1)
    factors_mine = lax.dynamic_slice_in_dim(factors, HALF * core, HALF, 0)
    factors_theirs = lax.dynamic_slice_in_dim(factors, HALF * (1 - core), HALF, 0)
    factors_pair = jnp.stack([factors_mine, lax.ppermute(factors_theirs, "ctx", SWAP)])
    factor_list = [factors_pair] + [
        lax.ppermute(factors_pair, "ctx", chips(step)) for step in range(1, NEIGH)
    ]
    q_other = lax.ppermute(q_theirs, "ctx", SWAP)

    pairs = [jnp.stack([kv_mine[h], kv_other[h]]) for h in range(HALF)]
    previous = [lax.ppermute(pairs[h], "ctx", plane(1)) for h in range(HALF)]
    blocks = []
    for h in range(HALF):
        arrived = [
            lax.ppermute(
                jnp.where(z + step >= 4, previous[h], pairs[h]), "ctx", along_z(step)
            )
            for step in range(1, 4)
        ]
        blocks.append([pairs[h], *arrived, previous[h]])

    def columns_of(half, step):
        target = (group + step) % N_HEAD
        block = lax.dynamic_slice(
            w_out, (half * HALF * DH, target * ROWS), (HALF * DH, ROWS)
        )
        return block.reshape(HALF, DH, ROWS)

    weights = [(columns_of(core, 0), columns_of(1 - core, 0))]
    for step in range(1, N_HEAD):
        fetched = lax.ppermute(columns_of(core, step), "head", along_y(step))
        weights.append((fetched, lax.ppermute(fetched, "ctx", SWAP)))

    turn = turns(core_array, factor_list)
    atts = [[] for _ in range(N_HEAD)]
    for h in range(HALF):
        both = attend(h, info, q_mine, q_other, turn, blocks[h])
        rows = jnp.stack([both[0], lax.ppermute(both[1], "ctx", SWAP)])
        atts[0].append(rows)
        for step in range(1, N_HEAD):
            atts[step].append(lax.ppermute(rows, "head", along_y(step)))
    total = project([a[:2] for a in atts], weights, 0, None, f32)
    total = project([a[2:3] for a in atts], weights, 2, total, f32)
    return project([a[3:] for a in atts], weights, 3, total, bf16)


def solution(mesh):
    spec = P("ctx", "head")
    return jax.shard_map(
        program,
        mesh=mesh,
        in_specs=(
            spec,
            spec,
            spec,
            P("ctx", "head", None, None),
            P("ctx", "head", None),
            P("ctx"),
            P("ctx", None),
            P("ctx"),
            P("head", None),
        ),
        out_specs=spec,
        check_vma=False,
    )
```

```python
import functools

import jax
import jax.numpy as jnp
from jax import lax
from jax.experimental import pallas as pl
from jax.experimental.pallas import tpu as pltpu
from jax.sharding import PartitionSpec as P

N_CTX = 32
N_HEAD = 4
HALF = 4
DH = 128
SHARD = 384
ROWS = 1024
QB = 256
NQB = 4
RANK = 64
CHAIN = 9
SUB = 16
BAND = 512
NEIGH = 5
LOG2E = 1.4426950408889634
SCALE = float(DH ** (-0.5) * LOG2E)
bf16 = jnp.bfloat16
f32 = jnp.float32


SWAP = [(s, s ^ 1) for s in range(N_CTX)]


def plane(step):
    return [(s, (s + 8 * step) % N_CTX) for s in range(N_CTX)]


def along_z(step):
    return [(s, (s // 8) * 8 + (s + 2 * step) % 8) for s in range(N_CTX)]


def along_y(step):
    return [(s, (s + step) % N_HEAD) for s in range(N_HEAD)]


def split(value):
    high = value.astype(bf16)
    low = (value - high.astype(f32)).astype(bf16)
    return high, low


def dot3(left, right, dims):
    def dot(a, b):
        return lax.dot_general(a, b, (dims, ((), ())), preferred_element_type=f32)

    left_high, left_low = split(left)
    right_high, right_low = split(right)
    return dot(left_high, right_high) + (dot(left_high, right_low) + dot(left_low, right_high))


def pack_kernel(core_ref, km, kt, vm, vt, qm, qt, kv_mine, kv_theirs, q_mine, q_theirs):
    for key, value, out in ((km, vm, kv_mine), (kt, vt, kv_theirs)):
        for part in range(3):
            rows = pl.ds(part * DH, DH)
            out[0, 0, part] = key[rows, :]
            out[0, 1, part] = value[rows, :].T
    q_mine[0] = qm[...]
    q_theirs[0] = qt[...]


def pack(core, keys, values, queries):
    def mine(h, c):
        return (0, HALF * c[0] + h)

    def theirs(h, c):
        return (0, HALF * (1 - c[0]) + h)

    kv_out = pl.BlockSpec((1, 2, 3, DH, DH), lambda h, c: (h, 0, 0, 0, 0))
    q_out = pl.BlockSpec((1, ROWS, DH), lambda h, c: (h, 0, 0))
    in_specs = []
    for rows in (SHARD, SHARD, ROWS):
        in_specs += [pl.BlockSpec((rows, DH), mine), pl.BlockSpec((rows, DH), theirs)]
    kv_shape = jax.ShapeDtypeStruct((HALF, 2, 3, DH, DH), bf16)
    q_shape = jax.ShapeDtypeStruct((HALF, ROWS, DH), bf16)
    return pl.pallas_call(
        pack_kernel,
        out_shape=(kv_shape, kv_shape, q_shape, q_shape),
        grid_spec=pltpu.PrefetchScalarGridSpec(
            num_scalar_prefetch=1,
            grid=(HALF,),
            in_specs=in_specs,
            out_specs=(kv_out, kv_out, q_out, q_out),
        ),
        name="pack",
    )(core, keys, keys, values, values, queries, queries)


def turns_kernel(core_ref, r0, r1, r2, r3, r4, out):
    core = core_ref[0]
    sources = (r0, r1, r2, r3, r4)
    row = lax.broadcasted_iota(jnp.int32, (RANK, RANK), 0)
    col = lax.broadcasted_iota(jnp.int32, (RANK, RANK), 1)
    big_row = lax.broadcasted_iota(jnp.int32, (DH, DH), 0)
    big_col = lax.broadcasted_iota(jnp.int32, (DH, DH), 1)
    eye = jnp.where(big_row == big_col, 1.0, 0.0).astype(f32)
    backs = []
    for items in (range(CHAIN),):
        units, lowers, solving = [], [], []
        for item in items:
            slot = (1 - item % 2) ^ core
            data = sources[item // 2][slot, 0].astype(f32)
            rows = data[:RANK]
            unit = rows / jnp.sqrt(jnp.sum(rows * rows, axis=-1, keepdims=True) + 1e-06)
            rates = data[RANK : RANK + 1, :RANK]
            rate = jnp.sum(jnp.where(row == col, rates, 0.0), axis=1, keepdims=True)
            gram = dot3(unit, unit, ((1,), (1,)))
            units.append(unit)
            lowers.append(rate * jnp.where(row > col, gram, 0.0))
            scaled = rate * unit
            solving.append([scaled[SUB * i : SUB * i + SUB] for i in range(RANK // SUB)])
        for block in range(RANK // SUB):
            at = SUB * block
            for lower, pieces in zip(lowers, solving):
                upper, under = pieces[block][:8], pieces[block][8:]
                for j in range(SUB - 1):
                    here = upper[j : j + 1] if j < 8 else under[j - 8 : j - 7]
                    if j < 7:
                        upper = upper - lower[at : at + 8, at + j : at + j + 1] * here
                    under = under - lower[at + 8 : at + 16, at + j : at + j + 1] * here
                pieces[block] = jnp.concatenate([upper, under], axis=0)
            if block + 1 < RANK // SUB:
                for lower, pieces in zip(lowers, solving):
                    change = dot3(
                        lower[at + SUB :, at : at + SUB], pieces[block], ((1,), (0,))
                    )
                    for i in range(block + 1, RANK // SUB):
                        first = SUB * (i - block - 1)
                        pieces[i] = pieces[i] - change[first : first + SUB]
        for unit, pieces in zip(units, solving):
            solved = jnp.concatenate(pieces, axis=0)
            backs.append(eye - dot3(unit, solved, ((0,), (0,))))
    for parity in range(2):
        high, low = split(eye * SCALE)
        out[parity ^ core, 0, 0, :DH, :] = high
        out[parity ^ core, 0, 0, DH:, :] = low
        total = backs[1 - parity]
        for m in range(1, CHAIN):
            if m > 1:
                total = dot3(backs[m - parity], total, ((1,), (0,)))
            high, low = split(total * SCALE)
            out[parity ^ core, 0, m, :DH, :] = high
            out[parity ^ core, 0, m, DH:, :] = low


def turns(core, factors, first, count):
    spec = pl.BlockSpec((2, 1, 80, DH), lambda h, c: (0, first + h, 0, 0))
    return pl.pallas_call(
        turns_kernel,
        out_shape=jax.ShapeDtypeStruct((2, count, CHAIN, 2 * DH, DH), bf16),
        grid_spec=pltpu.PrefetchScalarGridSpec(
            num_scalar_prefetch=1,
            grid=(count,),
            in_specs=[spec] * NEIGH,
            out_specs=pl.BlockSpec((2, 1, CHAIN, 2 * DH, DH), lambda h, c: (0, h, 0, 0, 0)),
        ),
    )(core, *factors)


def attend_kernel(
    info, qm, qt, turn, kv0, kv1, kv2, kv3, kv4, out, keys, vals, q_cols, top, best,
    score, acc,
):
    request = pl.program_id(0)
    core = info[0]
    parity = core ^ request
    base = 1 + 8 * request
    length = info[base]
    live = info[base + 1]

    @pl.when(request == 0)
    def _():
        q_cols[...] = qm[0].T

    @pl.when(request == 1)
    def _():
        q_cols[...] = qt[0].T

    for near, source in enumerate((kv0, kv1, kv2, kv3, kv4)):
        for slot in range(2):
            step = 2 * near - (slot ^ core) + parity

            @pl.when((step >= 0) & (step < length))
            def _():
                block = source[slot, 0].reshape(SHARD, DH)
                for part in range(3):
                    vals[step, :DH, part * DH : (part + 1) * DH] = source[slot, 1, part]
                vals[step, DH:, :] = jnp.ones((16, SHARD), bf16)

                doubled = jnp.concatenate([block, block], axis=1)
                keys[step] = jnp.dot(
                    doubled, turn[0, 0, step], preferred_element_type=f32
                ).astype(bf16)

    key_index = lax.broadcasted_iota(jnp.int32, (DH, QB), 0)
    lane = lax.broadcasted_iota(jnp.int32, (1, QB), 1)

    def scored(step, tile, buffer, kind, part, high):
        rows = pl.ds(part * DH, DH)
        found = jnp.dot(
            keys[step, rows, :], q_cols[:, tile * QB : (tile + 1) * QB],
            preferred_element_type=f32,
        )
        if kind == "home":
            position = info[base + 2 + tile] + lane - part * DH
            found = jnp.where(key_index <= position, found, -jnp.inf)
        elif kind == "oldest":
            found = jnp.where(key_index >= SHARD - live - part * DH, found, -jnp.inf)
        score[buffer, rows, :] = found
        best = jnp.max(found.reshape(DH // 8, 8, QB), axis=0)
        return best if high is None else jnp.maximum(high, best)

    def both(ahead, behind):
        high = None
        if behind is not None:
            step, tile, buffer, first = behind
            block = best[buffer]
            if first:
                limit = block
            else:
                before = top[tile]
                limit = jnp.maximum(before, block)
            parts = []
        for part in range(3):
            if ahead is not None:
                high = scored(*ahead, part, high)
            if behind is not None:
                rows = pl.ds(part * DH, DH)
                parts.append(jnp.exp2(score[buffer, rows, :] - limit).astype(bf16))
        if behind is not None:
            part = jnp.dot(
                vals[step], jnp.concatenate(parts, axis=0), preferred_element_type=f32
            )
            top[tile] = limit
            acc[tile] = part if first else acc[tile] * jnp.exp2(before - limit) + part
        if ahead is not None:
            best[ahead[2]] = jnp.max(high, axis=0, keepdims=True)

    order = [(0, tile, "home") for tile in range(NQB)]
    order += [(length - 1, tile, "oldest") for tile in range(NQB)]
    order += [(1, 0, "whole")]
    for at in range(len(order)):
        ahead = (order[at][0], order[at][1], at % 2, order[at][2])
        behind = None
        if at:
            behind = (order[at - 1][0], order[at - 1][1], (at - 1) % 2, at <= NQB)
        both(ahead, behind)

    def inner(step, carry):
        for tile in range(NQB):
            if tile + 1 < NQB:
                ahead = (step, tile + 1, (tile + 1) % 2, "whole")
            else:
                ahead = (jnp.minimum(step + 1, length - 2), 0, 0, "whole")
            both(ahead, (step, tile, tile % 2, False))
        return carry

    lax.fori_loop(1, length - 1, inner, 0)
    for tile in range(NQB):
        done = acc[tile, :DH] / acc[tile, DH : DH + 1]
        out[0, tile * QB : (tile + 1) * QB, :] = done.T.astype(bf16)


def attend(head, info, q_mine, q_theirs, turn, place, blocks):
    whole = pl.BlockSpec((2, 2, 3, DH, DH), lambda r, c: (0, 0, 0, 0, 0))
    q_spec = pl.BlockSpec((1, ROWS, DH), lambda r, c: (head, 0, 0))
    return pl.pallas_call(
        attend_kernel,
        out_shape=jax.ShapeDtypeStruct((2, ROWS, DH), bf16),
        grid_spec=pltpu.PrefetchScalarGridSpec(
            num_scalar_prefetch=1,
            grid=(2,),
            in_specs=[
                q_spec,
                q_spec,
                pl.BlockSpec(
                    (1, 1, CHAIN, 2 * DH, DH), lambda r, c: (r, place, 0, 0, 0)
                ),
            ]
            + [whole] * NEIGH,
            out_specs=pl.BlockSpec((1, ROWS, DH), lambda r, c: (r, 0, 0)),
            scratch_shapes=[
                pltpu.VMEM((CHAIN, SHARD, DH), bf16),
                pltpu.VMEM((CHAIN, DH + 16, SHARD), bf16),
                pltpu.VMEM((DH, ROWS), bf16),
                pltpu.VMEM((NQB, 1, QB), f32),
                pltpu.VMEM((2, 1, QB), f32),
                pltpu.VMEM((2, SHARD, QB), f32),
                pltpu.VMEM((NQB, DH + 16, QB), f32),
            ],
        ),
    )(info, q_mine, q_theirs, turn, *blocks)


def project_kernel(count, last, *refs):
    inputs = 4 * (2 * count + 2)
    atts = refs[: 8 * count]
    weights = refs[8 * count : inputs]
    rest = refs[inputs:]
    total = rest[0][...] if last else None
    for source in range(4):
        pair = [
            jnp.concatenate(
                [atts[2 * (source * count + h) + slot][0] for h in range(count)], axis=1
            )
            for slot in range(2)
        ]
        matrices = [
            weights[2 * source + slot][...].reshape(count * DH, -1) for slot in range(2)
        ]
        part = jnp.dot(
            jnp.concatenate(pair, axis=1),
            jnp.concatenate(matrices, axis=0),
            preferred_element_type=f32,
        )
        total = part if total is None else total + part
    rest[-1][...] = total.astype(rest[-1].dtype)


def project(atts, weights, first, total, dtype):
    count = len(atts[0])
    flat = [array for source in atts for both in source for array in both]
    flat_weights = [array for source in weights for array in source]
    att_specs = [
        pl.BlockSpec((1, BAND, DH), lambda r: (0, r, 0)),
        pl.BlockSpec((1, BAND, DH), lambda r: (1, r, 0)),
    ]
    weight_spec = pl.BlockSpec((count, DH, ROWS), lambda r: (first // count, 0, 0))
    total_spec = pl.BlockSpec((BAND, ROWS), lambda r: (r, 0))
    return pl.pallas_call(
        functools.partial(project_kernel, count, total is not None),
        out_shape=jax.ShapeDtypeStruct((ROWS, ROWS), dtype),
        grid=(ROWS // BAND,),
        in_specs=att_specs * (len(flat) // 2)
        + [weight_spec] * len(flat_weights)
        + ([total_spec] if total is not None else []),
        out_specs=total_spec,
    )(*flat, *flat_weights, *(() if total is None else (total,)))


def program(
    queries, cache_keys, cache_values, reflect, betas, chain_len, block_start, live_len, w_out
):
    here = lax.axis_index("ctx")
    group = lax.axis_index("head")
    core = here % 2
    z = (here % 8) // 2
    core_array = core[None].astype(jnp.int32)

    own_info = jnp.concatenate(
        [chain_len, live_len, block_start[0], jnp.zeros((2,), jnp.int32)]
    )
    info = jnp.concatenate([core_array, own_info, lax.ppermute(own_info, "ctx", SWAP)])

    kv_mine, kv_theirs, q_mine, q_theirs = pack(core_array, cache_keys, cache_values, queries)
    kv_other = lax.ppermute(kv_theirs, "ctx", SWAP)

    rates = jnp.pad(betas[0][:, None, :], ((0, 0), (0, 15), (0, DH - RANK)))
    factors = jnp.concatenate([reflect[0], rates], axis=1)
    factors_mine = lax.dynamic_slice_in_dim(factors, HALF * core, HALF, 0)
    factors_theirs = lax.dynamic_slice_in_dim(factors, HALF * (1 - core), HALF, 0)
    factors_pair = jnp.stack([factors_mine, lax.ppermute(factors_theirs, "ctx", SWAP)])
    factors_previous = lax.ppermute(factors_pair, "ctx", plane(1))
    factor_list = [factors_pair]
    for step in range(1, 4):
        chosen = jnp.where(z + step >= 4, factors_previous, factors_pair)
        factor_list.append(lax.ppermute(chosen, "ctx", along_z(step)))
    factor_list.append(factors_previous)
    q_other = lax.ppermute(q_theirs, "ctx", SWAP)

    pairs = [jnp.stack([kv_mine[h], kv_other[h]]) for h in range(HALF)]
    previous = [lax.ppermute(pairs[h], "ctx", plane(1)) for h in range(HALF)]
    blocks = []
    for h in range(HALF):
        arrived = [
            lax.ppermute(
                jnp.where(z + step >= 4, previous[h], pairs[h]), "ctx", along_z(step)
            )
            for step in range(1, 4)
        ]
        blocks.append([pairs[h], *arrived, previous[h]])

    def columns_of(half, step):
        target = (group + step) % N_HEAD
        block = lax.dynamic_slice(
            w_out, (half * HALF * DH, target * ROWS), (HALF * DH, ROWS)
        )
        return block.reshape(HALF, DH, ROWS)

    weights = [(columns_of(core, 0), columns_of(1 - core, 0))]
    for step in range(1, N_HEAD):
        fetched = lax.ppermute(columns_of(core, step), "head", along_y(step))
        weights.append((fetched, lax.ppermute(fetched, "ctx", SWAP)))

    turn_first = turns(core_array, factor_list, 0, 1)
    turn_rest = turns(core_array, factor_list, 1, HALF - 1)
    atts = [[] for _ in range(N_HEAD)]
    for h in range(HALF):
        turn, place = (turn_rest, h - 1) if h else (turn_first, 0)
        rows = attend(h, info, q_mine, q_other, turn, place, blocks[h])
        late = h < HALF - 1
        if not late:
            rows = jnp.stack([rows[0], lax.ppermute(rows[1], "ctx", SWAP)])
        for step in range(N_HEAD):
            piece = rows
            if step:
                piece = lax.ppermute(rows, "head", along_y(step))
            other = lax.ppermute(piece, "ctx", SWAP) if late else piece
            atts[step].append((piece, other))
    total = project([a[:3] for a in atts], weights, 0, None, f32)
    return project([a[3:] for a in atts], weights, 3, total, bf16)


def solution(mesh):
    spec = P("ctx", "head")
    return jax.shard_map(
        program,
        mesh=mesh,
        in_specs=(
            spec,
            spec,
            spec,
            P("ctx", "head", None, None),
            P("ctx", "head", None),
            P("ctx"),
            P("ctx", None),
            P("ctx"),
            P("head", None),
        ),
        out_specs=spec,
        check_vma=False,
    )
```

```python
import functools

import jax
import jax.numpy as jnp
from jax import lax
from jax.experimental import pallas as pl
from jax.experimental.pallas import tpu as pltpu
from jax.sharding import PartitionSpec as P

N_CTX = 32
N_HEAD = 4
HALF = 4
DH = 128
SHARD = 384
ROWS = 1024
QB = 256
NQB = 4
RANK = 64
CHAIN = 9
AHEAD = 3
PART = 192
SUB = 16
BAND = 512
NEIGH = 5
LOG2E = 1.4426950408889634
SCALE = float(DH ** (-0.5) * LOG2E)
bf16 = jnp.bfloat16
f32 = jnp.float32


SWAP = [(s, s ^ 1) for s in range(N_CTX)]


def plane(step):
    return [(s, (s + 8 * step) % N_CTX) for s in range(N_CTX)]


def along_z(step):
    return [(s, (s // 8) * 8 + (s + 2 * step) % 8) for s in range(N_CTX)]


def along_y(step):
    return [(s, (s + step) % N_HEAD) for s in range(N_HEAD)]


def split(value):
    high = value.astype(bf16)
    low = (value - high.astype(f32)).astype(bf16)
    return high, low


def dot3(left, right, dims):
    def dot(a, b):
        return lax.dot_general(a, b, (dims, ((), ())), preferred_element_type=f32)

    left_high, left_low = split(left)
    right_high, right_low = split(right)
    return dot(left_high, right_high) + (dot(left_high, right_low) + dot(left_low, right_high))


def pack_kernel(core_ref, km, kt, vm, vt, qm, qt, kv_mine, kv_theirs, q_mine, q_theirs):
    for key, value, out in ((km, vm, kv_mine), (kt, vt, kv_theirs)):
        for part in range(3):
            rows = pl.ds(part * DH, DH)
            out[0, 0, part] = key[rows, :]
            out[0, 1, part] = value[rows, :].T
    q_mine[0] = qm[...]
    q_theirs[0] = qt[...]


def pack(core, keys, values, queries):
    def mine(h, c):
        return (0, HALF * c[0] + h)

    def theirs(h, c):
        return (0, HALF * (1 - c[0]) + h)

    kv_out = pl.BlockSpec((1, 2, 3, DH, DH), lambda h, c: (h, 0, 0, 0, 0))
    q_out = pl.BlockSpec((1, ROWS, DH), lambda h, c: (h, 0, 0))
    in_specs = []
    for rows in (SHARD, SHARD, ROWS):
        in_specs += [pl.BlockSpec((rows, DH), mine), pl.BlockSpec((rows, DH), theirs)]
    kv_shape = jax.ShapeDtypeStruct((HALF, 2, 3, DH, DH), bf16)
    q_shape = jax.ShapeDtypeStruct((HALF, ROWS, DH), bf16)
    return pl.pallas_call(
        pack_kernel,
        out_shape=(kv_shape, kv_shape, q_shape, q_shape),
        grid_spec=pltpu.PrefetchScalarGridSpec(
            num_scalar_prefetch=1,
            grid=(HALF,),
            in_specs=in_specs,
            out_specs=(kv_out, kv_out, q_out, q_out),
        ),
        name="pack",
    )(core, keys, keys, values, values, queries, queries)


def turns_kernel(core_ref, r0, r1, r2, r3, r4, out):
    core = core_ref[0]
    sources = (r0, r1, r2, r3, r4)
    row = lax.broadcasted_iota(jnp.int32, (RANK, RANK), 0)
    col = lax.broadcasted_iota(jnp.int32, (RANK, RANK), 1)
    big_row = lax.broadcasted_iota(jnp.int32, (DH, DH), 0)
    big_col = lax.broadcasted_iota(jnp.int32, (DH, DH), 1)
    eye = jnp.where(big_row == big_col, 1.0, 0.0).astype(f32)
    backs = []
    for items in (range(CHAIN),):
        units, lowers, solving = [], [], []
        for item in items:
            slot = (1 - item % 2) ^ core
            data = sources[item // 2][slot, 0].astype(f32)
            rows = data[:RANK]
            unit = rows / jnp.sqrt(jnp.sum(rows * rows, axis=-1, keepdims=True) + 1e-06)
            rates = data[RANK : RANK + 1, :RANK]
            rate = jnp.sum(jnp.where(row == col, rates, 0.0), axis=1, keepdims=True)
            gram = dot3(unit, unit, ((1,), (1,)))
            units.append(unit)
            lowers.append(rate * jnp.where(row > col, gram, 0.0))
            scaled = rate * unit
            solving.append([scaled[SUB * i : SUB * i + SUB] for i in range(RANK // SUB)])
        for block in range(RANK // SUB):
            at = SUB * block
            for lower, pieces in zip(lowers, solving):
                upper, under = pieces[block][:8], pieces[block][8:]
                for j in range(SUB - 1):
                    here = upper[j : j + 1] if j < 8 else under[j - 8 : j - 7]
                    if j < 7:
                        upper = upper - lower[at : at + 8, at + j : at + j + 1] * here
                    under = under - lower[at + 8 : at + 16, at + j : at + j + 1] * here
                pieces[block] = jnp.concatenate([upper, under], axis=0)
            if block + 1 < RANK // SUB:
                for lower, pieces in zip(lowers, solving):
                    change = dot3(
                        lower[at + SUB :, at : at + SUB], pieces[block], ((1,), (0,))
                    )
                    for i in range(block + 1, RANK // SUB):
                        first = SUB * (i - block - 1)
                        pieces[i] = pieces[i] - change[first : first + SUB]
        for unit, pieces in zip(units, solving):
            solved = jnp.concatenate(pieces, axis=0)
            backs.append(eye - dot3(unit, solved, ((0,), (0,))))
    for parity in range(2):
        high, low = split(eye * SCALE)
        out[parity ^ core, 0, 0, :DH, :] = high
        out[parity ^ core, 0, 0, DH:, :] = low
        total = backs[1 - parity]
        for m in range(1, CHAIN):
            if m > 1:
                total = dot3(backs[m - parity], total, ((1,), (0,)))
            high, low = split(total * SCALE)
            out[parity ^ core, 0, m, :DH, :] = high
            out[parity ^ core, 0, m, DH:, :] = low


def turns(core, factors, first, count):
    spec = pl.BlockSpec((2, 1, 80, DH), lambda h, c: (0, first + h, 0, 0))
    return pl.pallas_call(
        turns_kernel,
        out_shape=jax.ShapeDtypeStruct((2, count, CHAIN, 2 * DH, DH), bf16),
        grid_spec=pltpu.PrefetchScalarGridSpec(
            num_scalar_prefetch=1,
            grid=(count,),
            in_specs=[spec] * NEIGH,
            out_specs=pl.BlockSpec((2, 1, CHAIN, 2 * DH, DH), lambda h, c: (0, h, 0, 0, 0)),
        ),
    )(core, *factors)


def attend_kernel(
    info, qm, qt, turn, kv0, kv1, kv2, kv3, kv4, out, keys, vals, q_cols, top, best,
    score, acc,
):
    request = pl.program_id(0)
    core = info[0]
    parity = core ^ request
    base = 1 + 8 * request
    length = info[base]
    live = info[base + 1]

    @pl.when(request == 0)
    def _():
        q_cols[...] = qm[0].T

    @pl.when(request == 1)
    def _():
        q_cols[...] = qt[0].T

    for near, source in enumerate((kv0, kv1, kv2, kv3, kv4)):
        for slot in range(2):
            step = 2 * near - (slot ^ core) + parity

            @pl.when((step >= 0) & (step < length))
            def _():
                block = source[slot, 0].reshape(SHARD, DH)
                for part in range(3):
                    vals[step, :DH, part * DH : (part + 1) * DH] = source[slot, 1, part]
                vals[step, DH:, :] = jnp.ones((16, SHARD), bf16)

                doubled = jnp.concatenate([block, block], axis=1)
                keys[step] = jnp.dot(
                    doubled, turn[0, 0, step], preferred_element_type=f32
                ).astype(bf16)

    key_index = lax.broadcasted_iota(jnp.int32, (PART, QB), 0)
    lane = lax.broadcasted_iota(jnp.int32, (1, QB), 1)

    def scored(step, tile, kind, part):
        found = jnp.dot(
            keys[step, pl.ds(part * PART, PART), :],
            q_cols[:, tile * QB : (tile + 1) * QB],
            preferred_element_type=f32,
        )
        if kind == "home":
            position = info[base + 2 + tile] + lane - part * PART
            found = jnp.where(key_index <= position, found, -jnp.inf)
        elif kind == "oldest":
            found = jnp.where(key_index >= SHARD - live - part * PART, found, -jnp.inf)
        return found

    def both(behind, ahead):
        high, parts = None, []
        if behind is not None:
            step, tile, kind = behind
            limit = best[tile]
            if kind != "home":
                before = top[tile]
                limit = jnp.maximum(before, limit)
        for part in range(SHARD // PART):
            rows = pl.ds(part * PART, PART)
            if ahead is not None:
                found = scored(*ahead, part)
                peak = jnp.max(found.reshape(PART // 8, 8, QB), axis=0)
                high = peak if high is None else jnp.maximum(high, peak)
            if behind is not None:
                parts.append(jnp.exp2(score[tile, rows, :] - limit).astype(bf16))
            if ahead is not None:
                score[ahead[1], rows, :] = found
        if behind is not None:
            summed = jnp.dot(
                vals[step], jnp.concatenate(parts, axis=0), preferred_element_type=f32
            )
            top[tile] = limit
            if kind == "home":
                acc[tile] = summed
            else:
                acc[tile] = acc[tile] * jnp.exp2(before - limit) + summed
        if ahead is not None:
            best[ahead[1]] = jnp.max(high, axis=0, keepdims=True)

    order = [(0, tile, "home") for tile in range(NQB)]
    order += [(length - 1, tile, "oldest") for tile in range(NQB)]
    count = len(order)
    order += [(1, tile, "whole") for tile in range(AHEAD)]
    for at in range(-AHEAD, count):
        both(order[at] if at >= 0 else None, order[at + AHEAD])

    def inner(step, carry):
        after = jnp.minimum(step + 1, length - 2)
        for tile in range(NQB):
            later = (tile + AHEAD) % NQB
            target = after if tile + AHEAD >= NQB else step
            both((step, tile, "whole"), (target, later, "whole"))
        return carry

    lax.fori_loop(1, length - 1, inner, 0)
    for tile in range(NQB):
        done = acc[tile, :DH] / acc[tile, DH : DH + 1]
        out[0, tile * QB : (tile + 1) * QB, :] = done.T.astype(bf16)


def attend(head, info, q_mine, q_theirs, turn, place, blocks):
    whole = pl.BlockSpec((2, 2, 3, DH, DH), lambda r, c: (0, 0, 0, 0, 0))
    q_spec = pl.BlockSpec((1, ROWS, DH), lambda r, c: (head, 0, 0))
    return pl.pallas_call(
        attend_kernel,
        out_shape=jax.ShapeDtypeStruct((2, ROWS, DH), bf16),
        grid_spec=pltpu.PrefetchScalarGridSpec(
            num_scalar_prefetch=1,
            grid=(2,),
            in_specs=[
                q_spec,
                q_spec,
                pl.BlockSpec(
                    (1, 1, CHAIN, 2 * DH, DH), lambda r, c: (r, place, 0, 0, 0)
                ),
            ]
            + [whole] * NEIGH,
            out_specs=pl.BlockSpec((1, ROWS, DH), lambda r, c: (r, 0, 0)),
            scratch_shapes=[
                pltpu.VMEM((CHAIN, SHARD, DH), bf16),
                pltpu.VMEM((CHAIN, DH + 16, SHARD), bf16),
                pltpu.VMEM((DH, ROWS), bf16),
                pltpu.VMEM((NQB, 1, QB), f32),
                pltpu.VMEM((NQB, 1, QB), f32),
                pltpu.VMEM((NQB, SHARD, QB), f32),
                pltpu.VMEM((NQB, DH + 16, QB), f32),
            ],
        ),
    )(info, q_mine, q_theirs, turn, *blocks)


def project_kernel(count, last, *refs):
    inputs = 4 * (2 * count + 2)
    atts = refs[: 8 * count]
    weights = refs[8 * count : inputs]
    rest = refs[inputs:]
    total = rest[0][...] if last else None
    for source in range(4):
        pair = [
            jnp.concatenate(
                [atts[2 * (source * count + h) + slot][0] for h in range(count)], axis=1
            )
            for slot in range(2)
        ]
        matrices = [
            weights[2 * source + slot][...].reshape(count * DH, -1) for slot in range(2)
        ]
        part = jnp.dot(
            jnp.concatenate(pair, axis=1),
            jnp.concatenate(matrices, axis=0),
            preferred_element_type=f32,
        )
        total = part if total is None else total + part
    rest[-1][...] = total.astype(rest[-1].dtype)


def project(atts, weights, first, total, dtype):
    count = len(atts[0])
    flat = [array for source in atts for both in source for array in both]
    flat_weights = [array for source in weights for array in source]
    att_specs = [
        pl.BlockSpec((1, BAND, DH), lambda r: (0, r, 0)),
        pl.BlockSpec((1, BAND, DH), lambda r: (1, r, 0)),
    ]
    weight_spec = pl.BlockSpec((count, DH, ROWS), lambda r: (first // count, 0, 0))
    total_spec = pl.BlockSpec((BAND, ROWS), lambda r: (r, 0))
    return pl.pallas_call(
        functools.partial(project_kernel, count, total is not None),
        out_shape=jax.ShapeDtypeStruct((ROWS, ROWS), dtype),
        grid=(ROWS // BAND,),
        in_specs=att_specs * (len(flat) // 2)
        + [weight_spec] * len(flat_weights)
        + ([total_spec] if total is not None else []),
        out_specs=total_spec,
    )(*flat, *flat_weights, *(() if total is None else (total,)))


def program(
    queries, cache_keys, cache_values, reflect, betas, chain_len, block_start, live_len, w_out
):
    here = lax.axis_index("ctx")
    group = lax.axis_index("head")
    core = here % 2
    z = (here % 8) // 2
    core_array = core[None].astype(jnp.int32)

    own_info = jnp.concatenate(
        [chain_len, live_len, block_start[0], jnp.zeros((2,), jnp.int32)]
    )
    info = jnp.concatenate([core_array, own_info, lax.ppermute(own_info, "ctx", SWAP)])

    kv_mine, kv_theirs, q_mine, q_theirs = pack(core_array, cache_keys, cache_values, queries)
    kv_other = lax.ppermute(kv_theirs, "ctx", SWAP)

    rates = jnp.pad(betas[0][:, None, :], ((0, 0), (0, 15), (0, DH - RANK)))
    factors = jnp.concatenate([reflect[0], rates], axis=1)
    factors_mine = lax.dynamic_slice_in_dim(factors, HALF * core, HALF, 0)
    factors_theirs = lax.dynamic_slice_in_dim(factors, HALF * (1 - core), HALF, 0)
    factors_pair = jnp.stack([factors_mine, lax.ppermute(factors_theirs, "ctx", SWAP)])
    factors_previous = lax.ppermute(factors_pair, "ctx", plane(1))
    factor_list = [factors_pair]
    for step in range(1, 4):
        chosen = jnp.where(z + step >= 4, factors_previous, factors_pair)
        factor_list.append(lax.ppermute(chosen, "ctx", along_z(step)))
    factor_list.append(factors_previous)
    q_other = lax.ppermute(q_theirs, "ctx", SWAP)

    pairs = [jnp.stack([kv_mine[h], kv_other[h]]) for h in range(HALF)]
    previous = [lax.ppermute(pairs[h], "ctx", plane(1)) for h in range(HALF)]
    blocks = []
    for h in range(HALF):
        picked = [
            jnp.where(z + step >= 4, previous[h], pairs[h]) for step in range(1, 4)
        ]
        arrived = [
            lax.ppermute(picked[step - 1], "ctx", along_z(step))
            for step in range(1, 4)
        ]
        blocks.append([pairs[h], *arrived, previous[h]])

    def columns_of(half, step):
        target = (group + step) % N_HEAD
        block = lax.dynamic_slice(
            w_out, (half * HALF * DH, target * ROWS), (HALF * DH, ROWS)
        )
        return block.reshape(HALF, DH, ROWS)

    weights = [(columns_of(core, 0), columns_of(1 - core, 0))]
    for step in range(1, N_HEAD):
        fetched = lax.ppermute(columns_of(core, step), "head", along_y(step))
        weights.append((fetched, lax.ppermute(fetched, "ctx", SWAP)))

    turn_first = turns(core_array, factor_list, 0, 1)
    turn_rest = turns(core_array, factor_list, 1, HALF - 1)
    atts = [[] for _ in range(N_HEAD)]
    for h in range(HALF):
        turn, place = (turn_rest, h - 1) if h else (turn_first, 0)
        rows = attend(h, info, q_mine, q_other, turn, place, blocks[h])
        late = h < HALF - 1
        if not late:
            rows = jnp.stack([rows[0], lax.ppermute(rows[1], "ctx", SWAP)])
        for step in range(N_HEAD):
            piece = rows
            if step:
                piece = lax.ppermute(rows, "head", along_y(step))
            other = lax.ppermute(piece, "ctx", SWAP) if late else piece
            atts[step].append((piece, other))
    total = project([a[:3] for a in atts], weights, 0, None, f32)
    return project([a[3:] for a in atts], weights, 3, total, bf16)


def solution(mesh):
    spec = P("ctx", "head")
    return jax.shard_map(
        program,
        mesh=mesh,
        in_specs=(
            spec,
            spec,
            spec,
            P("ctx", "head", None, None),
            P("ctx", "head", None),
            P("ctx"),
            P("ctx", None),
            P("ctx"),
            P("head", None),
        ),
        out_specs=spec,
        check_vma=False,
    )
```

```python
import functools

import jax
import jax.numpy as jnp
from jax import lax
from jax.experimental import pallas as pl
from jax.experimental.pallas import tpu as pltpu
from jax.sharding import PartitionSpec as P

N_CTX = 32
N_HEAD = 4
HALF = 4
DH = 128
SHARD = 384
ROWS = 1024
QB = 256
NQB = 4
RANK = 64
CHAIN = 9
AHEAD = 3
PART = 192
SUB = 16
BAND = 256
NEIGH = 5
LOG2E = 1.4426950408889634
SCALE = float(DH ** (-0.5) * LOG2E)
bf16 = jnp.bfloat16
f32 = jnp.float32


SWAP = [(s, s ^ 1) for s in range(N_CTX)]


def plane(step):
    return [(s, (s + 8 * step) % N_CTX) for s in range(N_CTX)]


def along_z(step):
    return [(s, (s // 8) * 8 + (s + 2 * step) % 8) for s in range(N_CTX)]


def along_y(step):
    return [(s, (s + step) % N_HEAD) for s in range(N_HEAD)]


def split(value):
    high = value.astype(bf16)
    low = (value - high.astype(f32)).astype(bf16)
    return high, low


def dot3(left, right, dims):
    def dot(a, b):
        return lax.dot_general(a, b, (dims, ((), ())), preferred_element_type=f32)

    left_high, left_low = split(left)
    right_high, right_low = split(right)
    return dot(left_high, right_high) + (dot(left_high, right_low) + dot(left_low, right_high))


def pack_kernel(core_ref, km, kt, vm, vt, qm, qt, kv_mine, kv_theirs, q_mine, q_theirs):
    for key, value, out in ((km, vm, kv_mine), (kt, vt, kv_theirs)):
        for part in range(3):
            rows = pl.ds(part * DH, DH)
            out[0, 0, part] = key[rows, :]
            out[0, 1, part] = value[rows, :].T
    q_mine[0] = qm[...]
    q_theirs[0] = qt[...]


def pack(core, keys, values, queries):
    def mine(h, c):
        return (0, HALF * c[0] + h)

    def theirs(h, c):
        return (0, HALF * (1 - c[0]) + h)

    kv_out = pl.BlockSpec((1, 2, 3, DH, DH), lambda h, c: (h, 0, 0, 0, 0))
    q_out = pl.BlockSpec((1, ROWS, DH), lambda h, c: (h, 0, 0))
    in_specs = []
    for rows in (SHARD, SHARD, ROWS):
        in_specs += [pl.BlockSpec((rows, DH), mine), pl.BlockSpec((rows, DH), theirs)]
    kv_shape = jax.ShapeDtypeStruct((HALF, 2, 3, DH, DH), bf16)
    q_shape = jax.ShapeDtypeStruct((HALF, ROWS, DH), bf16)
    return pl.pallas_call(
        pack_kernel,
        out_shape=(kv_shape, kv_shape, q_shape, q_shape),
        grid_spec=pltpu.PrefetchScalarGridSpec(
            num_scalar_prefetch=1,
            grid=(HALF,),
            in_specs=in_specs,
            out_specs=(kv_out, kv_out, q_out, q_out),
        ),
        name="pack",
    )(core, keys, keys, values, values, queries, queries)


def turns_kernel(core_ref, r0, r1, r2, r3, r4, out):
    core = core_ref[0]
    sources = (r0, r1, r2, r3, r4)
    row = lax.broadcasted_iota(jnp.int32, (RANK, RANK), 0)
    col = lax.broadcasted_iota(jnp.int32, (RANK, RANK), 1)
    big_row = lax.broadcasted_iota(jnp.int32, (DH, DH), 0)
    big_col = lax.broadcasted_iota(jnp.int32, (DH, DH), 1)
    eye = jnp.where(big_row == big_col, 1.0, 0.0).astype(f32)
    backs = []
    for items in (range(CHAIN),):
        units, lowers, solving = [], [], []
        for item in items:
            slot = (1 - item % 2) ^ core
            data = sources[item // 2][slot, 0].astype(f32)
            rows = data[:RANK]
            unit = rows / jnp.sqrt(jnp.sum(rows * rows, axis=-1, keepdims=True) + 1e-06)
            rates = data[RANK : RANK + 1, :RANK]
            rate = jnp.sum(jnp.where(row == col, rates, 0.0), axis=1, keepdims=True)
            gram = dot3(unit, unit, ((1,), (1,)))
            units.append(unit)
            lowers.append(rate * jnp.where(row > col, gram, 0.0))
            scaled = rate * unit
            solving.append([scaled[SUB * i : SUB * i + SUB] for i in range(RANK // SUB)])
        for block in range(RANK // SUB):
            at = SUB * block
            for lower, pieces in zip(lowers, solving):
                upper, under = pieces[block][:8], pieces[block][8:]
                for j in range(SUB - 1):
                    here = upper[j : j + 1] if j < 8 else under[j - 8 : j - 7]
                    if j < 7:
                        upper = upper - lower[at : at + 8, at + j : at + j + 1] * here
                    under = under - lower[at + 8 : at + 16, at + j : at + j + 1] * here
                pieces[block] = jnp.concatenate([upper, under], axis=0)
            if block + 1 < RANK // SUB:
                for lower, pieces in zip(lowers, solving):
                    change = dot3(
                        lower[at + SUB :, at : at + SUB], pieces[block], ((1,), (0,))
                    )
                    for i in range(block + 1, RANK // SUB):
                        first = SUB * (i - block - 1)
                        pieces[i] = pieces[i] - change[first : first + SUB]
        for unit, pieces in zip(units, solving):
            solved = jnp.concatenate(pieces, axis=0)
            backs.append(eye - dot3(unit, solved, ((0,), (0,))))
    for parity in range(2):
        high, low = split(eye * SCALE)
        out[parity ^ core, 0, 0, :DH, :] = high
        out[parity ^ core, 0, 0, DH:, :] = low
        total = backs[1 - parity]
        for m in range(1, CHAIN):
            if m > 1:
                total = dot3(backs[m - parity], total, ((1,), (0,)))
            high, low = split(total * SCALE)
            out[parity ^ core, 0, m, :DH, :] = high
            out[parity ^ core, 0, m, DH:, :] = low


def turns(core, factors, first, count):
    spec = pl.BlockSpec((2, 1, 80, DH), lambda h, c: (0, first + h, 0, 0))
    return pl.pallas_call(
        turns_kernel,
        out_shape=jax.ShapeDtypeStruct((2, count, CHAIN, 2 * DH, DH), bf16),
        grid_spec=pltpu.PrefetchScalarGridSpec(
            num_scalar_prefetch=1,
            grid=(count,),
            in_specs=[spec] * NEIGH,
            out_specs=pl.BlockSpec((2, 1, CHAIN, 2 * DH, DH), lambda h, c: (0, h, 0, 0, 0)),
        ),
    )(core, *factors)


def attend_kernel(
    info, qm, qt, turn, kv0, kv1, kv2, kv3, kv4, out, keys, vals, q_cols, top, best,
    score, acc,
):
    request = pl.program_id(0)
    core = info[0]
    parity = core ^ request
    base = 1 + 8 * request
    length = info[base]
    live = info[base + 1]

    @pl.when(request == 0)
    def _():
        q_cols[...] = qm[0].T

    @pl.when(request == 1)
    def _():
        q_cols[...] = qt[0].T

    def ready(slot, near, source):
        step = 2 * near - (slot ^ core) + parity

        @pl.when((step >= 0) & (step < length))
        def _():
            block = source[slot, 0].reshape(SHARD, DH)
            for part in range(3):
                vals[step, :DH, part * DH : (part + 1) * DH] = source[slot, 1, part]
            vals[step, DH:, :] = jnp.ones((16, SHARD), bf16)
            doubled = jnp.concatenate([block, block], axis=1)
            keys[step] = jnp.dot(
                doubled, turn[0, 0, step], preferred_element_type=f32
            ).astype(bf16)

    for near, source in enumerate((kv0, kv1, kv2, kv3, kv4)):

        def chip(slot, carry):
            ready(slot, near, source)
            return carry

        lax.fori_loop(0, 2, chip, 0)

    key_index = lax.broadcasted_iota(jnp.int32, (PART, QB), 0)
    lane = lax.broadcasted_iota(jnp.int32, (1, QB), 1)

    def scored(step, tile, kind, part):
        found = jnp.dot(
            keys[step, pl.ds(part * PART, PART), :],
            q_cols[:, tile * QB : (tile + 1) * QB],
            preferred_element_type=f32,
        )
        if kind == "home":
            position = info[base + 2 + tile] + lane - part * PART
            found = jnp.where(key_index <= position, found, -jnp.inf)
        elif kind == "oldest":
            found = jnp.where(key_index >= SHARD - live - part * PART, found, -jnp.inf)
        return found

    def both(behind, ahead):
        high, parts = None, []
        if behind is not None:
            step, tile, kind = behind
            limit = best[tile]
            if kind != "home":
                before = top[tile]
                limit = jnp.maximum(before, limit)
        for part in range(SHARD // PART):
            rows = pl.ds(part * PART, PART)
            if ahead is not None:
                found = scored(*ahead, part)
                peak = jnp.max(found.reshape(PART // 8, 8, QB), axis=0)
                high = peak if high is None else jnp.maximum(high, peak)
            if behind is not None:
                parts.append(jnp.exp2(score[tile, rows, :] - limit).astype(bf16))
            if ahead is not None:
                score[ahead[1], rows, :] = found
        if behind is not None:
            summed = jnp.dot(
                vals[step], jnp.concatenate(parts, axis=0), preferred_element_type=f32
            )
            top[tile] = limit
            if kind == "home":
                acc[tile] = summed
            else:
                acc[tile] = acc[tile] * jnp.exp2(before - limit) + summed
        if ahead is not None:
            best[ahead[1]] = jnp.max(high, axis=0, keepdims=True)

    order = [(0, tile, "home") for tile in range(NQB)]
    order += [(length - 1, tile, "oldest") for tile in range(NQB)]
    count = len(order)
    order += [(1, tile, "whole") for tile in range(AHEAD)]
    for at in range(-AHEAD, count):
        both(order[at] if at >= 0 else None, order[at + AHEAD])

    def inner(step, carry):
        after = jnp.minimum(step + 1, length - 2)
        for tile in range(NQB):
            later = (tile + AHEAD) % NQB
            target = after if tile + AHEAD >= NQB else step
            both((step, tile, "whole"), (target, later, "whole"))
        return carry

    lax.fori_loop(1, length - 1, inner, 0)
    for tile in range(NQB):
        done = acc[tile, :DH] / acc[tile, DH : DH + 1]
        out[0, tile * QB : (tile + 1) * QB, :] = done.T.astype(bf16)


def attend(head, info, q_mine, q_theirs, turn, place, blocks):
    whole = pl.BlockSpec((2, 2, 3, DH, DH), lambda r, c: (0, 0, 0, 0, 0))
    q_spec = pl.BlockSpec((1, ROWS, DH), lambda r, c: (head, 0, 0))
    return pl.pallas_call(
        attend_kernel,
        out_shape=jax.ShapeDtypeStruct((2, ROWS, DH), bf16),
        grid_spec=pltpu.PrefetchScalarGridSpec(
            num_scalar_prefetch=1,
            grid=(2,),
            in_specs=[
                q_spec,
                q_spec,
                pl.BlockSpec(
                    (1, 1, CHAIN, 2 * DH, DH), lambda r, c: (r, place, 0, 0, 0)
                ),
            ]
            + [whole] * NEIGH,
            out_specs=pl.BlockSpec((1, ROWS, DH), lambda r, c: (r, 0, 0)),
            scratch_shapes=[
                pltpu.VMEM((CHAIN, SHARD, DH), bf16),
                pltpu.VMEM((CHAIN, DH + 16, SHARD), bf16),
                pltpu.VMEM((DH, ROWS), bf16),
                pltpu.VMEM((NQB, 1, QB), f32),
                pltpu.VMEM((NQB, 1, QB), f32),
                pltpu.VMEM((NQB, SHARD, QB), f32),
                pltpu.VMEM((NQB, DH + 16, QB), f32),
            ],
        ),
    )(info, q_mine, q_theirs, turn, *blocks)


def project_kernel(count, last, *refs):
    inputs = 4 * (2 * count + 2)
    atts = refs[: 8 * count]
    weights = refs[8 * count : inputs]
    rest = refs[inputs:]
    total = rest[0][...] if last else None
    for source in range(4):
        pair = [
            jnp.concatenate(
                [atts[2 * (source * count + h) + slot][0] for h in range(count)], axis=1
            )
            for slot in range(2)
        ]
        matrices = [
            weights[2 * source + slot][...].reshape(count * DH, -1) for slot in range(2)
        ]
        part = jnp.dot(
            jnp.concatenate(pair, axis=1),
            jnp.concatenate(matrices, axis=0),
            preferred_element_type=f32,
        )
        total = part if total is None else total + part
    rest[-1][...] = total.astype(rest[-1].dtype)


def project(atts, weights, first, total, dtype):
    count = len(atts[0])
    flat = [array for source in atts for both in source for array in both]
    flat_weights = [array for source in weights for array in source]
    att_specs = [
        pl.BlockSpec((1, BAND, DH), lambda r: (0, r, 0)),
        pl.BlockSpec((1, BAND, DH), lambda r: (1, r, 0)),
    ]
    weight_spec = pl.BlockSpec((count, DH, ROWS), lambda r: (first // count, 0, 0))
    total_spec = pl.BlockSpec((BAND, ROWS), lambda r: (r, 0))
    return pl.pallas_call(
        functools.partial(project_kernel, count, total is not None),
        out_shape=jax.ShapeDtypeStruct((ROWS, ROWS), dtype),
        grid=(ROWS // BAND,),
        in_specs=att_specs * (len(flat) // 2)
        + [weight_spec] * len(flat_weights)
        + ([total_spec] if total is not None else []),
        out_specs=total_spec,
    )(*flat, *flat_weights, *(() if total is None else (total,)))


def program(
    queries, cache_keys, cache_values, reflect, betas, chain_len, block_start, live_len, w_out
):
    here = lax.axis_index("ctx")
    group = lax.axis_index("head")
    core = here % 2
    z = (here % 8) // 2
    core_array = core[None].astype(jnp.int32)

    own_info = jnp.concatenate(
        [chain_len, live_len, block_start[0], jnp.zeros((2,), jnp.int32)]
    )
    info = jnp.concatenate([core_array, own_info, lax.ppermute(own_info, "ctx", SWAP)])

    kv_mine, kv_theirs, q_mine, q_theirs = pack(core_array, cache_keys, cache_values, queries)
    kv_other = lax.ppermute(kv_theirs, "ctx", SWAP)

    rates = jnp.pad(betas[0][:, None, :], ((0, 0), (0, 15), (0, DH - RANK)))
    factors = jnp.concatenate([reflect[0], rates], axis=1)
    factors_mine = lax.dynamic_slice_in_dim(factors, HALF * core, HALF, 0)
    factors_theirs = lax.dynamic_slice_in_dim(factors, HALF * (1 - core), HALF, 0)
    factors_pair = jnp.stack([factors_mine, lax.ppermute(factors_theirs, "ctx", SWAP)])
    factors_previous = lax.ppermute(factors_pair, "ctx", plane(1))
    factor_list = [factors_pair]
    for step in range(1, 4):
        chosen = jnp.where(z + step >= 4, factors_previous, factors_pair)
        factor_list.append(lax.ppermute(chosen, "ctx", along_z(step)))
    factor_list.append(factors_previous)
    q_other = lax.ppermute(q_theirs, "ctx", SWAP)

    pairs = [jnp.stack([kv_mine[h], kv_other[h]]) for h in range(HALF)]
    previous = [lax.ppermute(pairs[h], "ctx", plane(1)) for h in range(HALF)]
    blocks = []
    for h in range(HALF):
        picked = [
            jnp.where(z + step >= 4, previous[h], pairs[h]) for step in range(1, 4)
        ]
        arrived = [
            lax.ppermute(picked[step - 1], "ctx", along_z(step))
            for step in range(1, 4)
        ]
        blocks.append([pairs[h], *arrived, previous[h]])

    def columns_of(half, step):
        target = (group + step) % N_HEAD
        block = lax.dynamic_slice(
            w_out, (half * HALF * DH, target * ROWS), (HALF * DH, ROWS)
        )
        return block.reshape(HALF, DH, ROWS)

    weights = [(columns_of(core, 0), columns_of(1 - core, 0))]
    for step in range(1, N_HEAD):
        fetched = lax.ppermute(columns_of(core, step), "head", along_y(step))
        weights.append((fetched, lax.ppermute(fetched, "ctx", SWAP)))

    turn_first = turns(core_array, factor_list, 0, 1)
    turn_rest = turns(core_array, factor_list, 1, HALF - 1)
    atts = [[] for _ in range(N_HEAD)]
    for h in range(HALF):
        turn, place = (turn_rest, h - 1) if h else (turn_first, 0)
        rows = attend(h, info, q_mine, q_other, turn, place, blocks[h])
        late = h < HALF - 1
        if not late:
            rows = jnp.stack([rows[0], lax.ppermute(rows[1], "ctx", SWAP)])
        for step in range(N_HEAD):
            piece = rows
            if step:
                piece = lax.ppermute(rows, "head", along_y(step))
            other = lax.ppermute(piece, "ctx", SWAP) if late else piece
            atts[step].append((piece, other))
    total = project([a[:3] for a in atts], weights, 0, None, f32)
    return project([a[3:] for a in atts], weights, 3, total, bf16)


def solution(mesh):
    spec = P("ctx", "head")
    return jax.shard_map(
        program,
        mesh=mesh,
        in_specs=(
            spec,
            spec,
            spec,
            P("ctx", "head", None, None),
            P("ctx", "head", None),
            P("ctx"),
            P("ctx", None),
            P("ctx"),
            P("head", None),
        ),
        out_specs=spec,
        check_vma=False,
    )
```

```python
import functools

import jax
import jax.numpy as jnp
from jax import lax
from jax.experimental import pallas as pl
from jax.experimental.pallas import tpu as pltpu
from jax.sharding import PartitionSpec as P

N_CTX = 32
N_HEAD = 4
HALF = 4
DH = 128
SHARD = 384
ROWS = 1024
QB = 256
NQB = 4
RANK = 64
CHAIN = 9
AHEAD = 3
PART = 192
SUB = 16
BAND = 256
NEIGH = 5
LOG2E = 1.4426950408889634
SCALE = float(DH ** (-0.5) * LOG2E)
bf16 = jnp.bfloat16
f32 = jnp.float32


SWAP = [(s, s ^ 1) for s in range(N_CTX)]


def plane(step):
    return [(s, (s + 8 * step) % N_CTX) for s in range(N_CTX)]


def along_z(step):
    return [(s, (s // 8) * 8 + (s + 2 * step) % 8) for s in range(N_CTX)]


def along_y(step):
    return [(s, (s + step) % N_HEAD) for s in range(N_HEAD)]


def split(value):
    high = value.astype(bf16)
    low = (value - high.astype(f32)).astype(bf16)
    return high, low


def dot3(left, right, dims):
    def dot(a, b):
        return lax.dot_general(a, b, (dims, ((), ())), preferred_element_type=f32)

    left_high, left_low = split(left)
    right_high, right_low = split(right)
    return dot(left_high, right_high) + (dot(left_high, right_low) + dot(left_low, right_high))


def pack_kernel(core_ref, km, kt, vm, vt, qm, qt, kv_mine, kv_theirs, q_mine, q_theirs):
    for key, value, out in ((km, vm, kv_mine), (kt, vt, kv_theirs)):
        for part in range(3):
            rows = pl.ds(part * DH, DH)
            out[0, 0, part] = key[rows, :]
            out[0, 1, part] = value[rows, :].T
    q_mine[0] = qm[...]
    q_theirs[0] = qt[...]


def pack(core, keys, values, queries):
    def mine(h, c):
        return (0, HALF * c[0] + h)

    def theirs(h, c):
        return (0, HALF * (1 - c[0]) + h)

    kv_out = pl.BlockSpec((1, 2, 3, DH, DH), lambda h, c: (h, 0, 0, 0, 0))
    q_out = pl.BlockSpec((1, ROWS, DH), lambda h, c: (h, 0, 0))
    in_specs = []
    for rows in (SHARD, SHARD, ROWS):
        in_specs += [pl.BlockSpec((rows, DH), mine), pl.BlockSpec((rows, DH), theirs)]
    kv_shape = jax.ShapeDtypeStruct((HALF, 2, 3, DH, DH), bf16)
    q_shape = jax.ShapeDtypeStruct((HALF, ROWS, DH), bf16)
    return pl.pallas_call(
        pack_kernel,
        out_shape=(kv_shape, kv_shape, q_shape, q_shape),
        grid_spec=pltpu.PrefetchScalarGridSpec(
            num_scalar_prefetch=1,
            grid=(HALF,),
            in_specs=in_specs,
            out_specs=(kv_out, kv_out, q_out, q_out),
        ),
        name="pack",
    )(core, keys, keys, values, values, queries, queries)


def turns_kernel(core_ref, r0, r1, r2, r3, r4, out):
    core = core_ref[0]
    sources = (r0, r1, r2, r3, r4)
    row = lax.broadcasted_iota(jnp.int32, (RANK, RANK), 0)
    col = lax.broadcasted_iota(jnp.int32, (RANK, RANK), 1)
    big_row = lax.broadcasted_iota(jnp.int32, (DH, DH), 0)
    big_col = lax.broadcasted_iota(jnp.int32, (DH, DH), 1)
    eye = jnp.where(big_row == big_col, 1.0, 0.0).astype(f32)
    backs = []
    for items in (range(CHAIN),):
        units, lowers, solving = [], [], []
        for item in items:
            slot = (1 - item % 2) ^ core
            data = sources[item // 2][slot, 0].astype(f32)
            rows = data[:RANK]
            unit = rows / jnp.sqrt(jnp.sum(rows * rows, axis=-1, keepdims=True) + 1e-06)
            rates = data[RANK : RANK + 1, :RANK]
            rate = jnp.sum(jnp.where(row == col, rates, 0.0), axis=1, keepdims=True)
            gram = dot3(unit, unit, ((1,), (1,)))
            units.append(unit)
            lowers.append(rate * jnp.where(row > col, gram, 0.0))
            scaled = rate * unit
            solving.append([scaled[SUB * i : SUB * i + SUB] for i in range(RANK // SUB)])
        for block in range(RANK // SUB):
            at = SUB * block
            for lower, pieces in zip(lowers, solving):
                upper, under = pieces[block][:8], pieces[block][8:]
                for j in range(SUB - 1):
                    here = upper[j : j + 1] if j < 8 else under[j - 8 : j - 7]
                    if j < 7:
                        upper = upper - lower[at : at + 8, at + j : at + j + 1] * here
                    under = under - lower[at + 8 : at + 16, at + j : at + j + 1] * here
                pieces[block] = jnp.concatenate([upper, under], axis=0)
            if block + 1 < RANK // SUB:
                for lower, pieces in zip(lowers, solving):
                    change = dot3(
                        lower[at + SUB :, at : at + SUB], pieces[block], ((1,), (0,))
                    )
                    for i in range(block + 1, RANK // SUB):
                        first = SUB * (i - block - 1)
                        pieces[i] = pieces[i] - change[first : first + SUB]
        for unit, pieces in zip(units, solving):
            solved = jnp.concatenate(pieces, axis=0)
            backs.append(eye - dot3(unit, solved, ((0,), (0,))))
    for parity in range(2):
        high, low = split(eye * SCALE)
        out[parity ^ core, 0, 0, :DH, :] = high
        out[parity ^ core, 0, 0, DH:, :] = low
        total = backs[1 - parity]
        for m in range(1, CHAIN):
            if m > 1:
                total = dot3(backs[m - parity], total, ((1,), (0,)))
            high, low = split(total * SCALE)
            out[parity ^ core, 0, m, :DH, :] = high
            out[parity ^ core, 0, m, DH:, :] = low


def turns(core, factors, first, count):
    spec = pl.BlockSpec((2, 1, 80, DH), lambda h, c: (0, first + h, 0, 0))
    return pl.pallas_call(
        turns_kernel,
        out_shape=jax.ShapeDtypeStruct((2, count, CHAIN, 2 * DH, DH), bf16),
        grid_spec=pltpu.PrefetchScalarGridSpec(
            num_scalar_prefetch=1,
            grid=(count,),
            in_specs=[spec] * NEIGH,
            out_specs=pl.BlockSpec((2, 1, CHAIN, 2 * DH, DH), lambda h, c: (0, h, 0, 0, 0)),
        ),
    )(core, *factors)


def attend_kernel(
    info, qm, qt, turn, kv0, kv1, kv2, kv3, kv4, out, keys, vals, q_cols, top, best,
    score, acc,
):
    request = pl.program_id(0)
    core = info[0]
    parity = core ^ request
    base = 1 + 8 * request
    length = info[base]
    live = info[base + 1]

    def turned_rows(source, tile, carry):
        at = pl.ds(pl.multiple_of(tile * QB, QB), QB)
        q_cols[:, at] = source[0, at, :].T
        return carry

    @pl.when(request == 0)
    def _():
        lax.fori_loop(0, NQB, functools.partial(turned_rows, qm), 0)

    @pl.when(request == 1)
    def _():
        lax.fori_loop(0, NQB, functools.partial(turned_rows, qt), 0)

    def ready(slot, near, source):
        step = 2 * near - (slot ^ core) + parity

        @pl.when((step >= 0) & (step < length))
        def _():
            block = source[slot, 0].reshape(SHARD, DH)
            for part in range(3):
                vals[step, :DH, part * DH : (part + 1) * DH] = source[slot, 1, part]
            vals[step, DH:, :] = jnp.ones((16, SHARD), bf16)
            doubled = jnp.concatenate([block, block], axis=1)
            keys[step] = jnp.dot(
                doubled, turn[0, 0, step], preferred_element_type=f32
            ).astype(bf16)

    for near, source in enumerate((kv0, kv1, kv2, kv3, kv4)):

        def chip(slot, carry):
            ready(slot, near, source)
            return carry

        lax.fori_loop(0, 2, chip, 0)

    key_index = lax.broadcasted_iota(jnp.int32, (PART, QB), 0)
    lane = lax.broadcasted_iota(jnp.int32, (1, QB), 1)

    def scored(step, tile, kind, part):
        found = jnp.dot(
            keys[step, pl.ds(part * PART, PART), :],
            q_cols[:, tile * QB : (tile + 1) * QB],
            preferred_element_type=f32,
        )
        if kind == "home":
            position = info[base + 2 + tile] + lane - part * PART
            found = jnp.where(key_index <= position, found, -jnp.inf)
        elif kind == "oldest":
            found = jnp.where(key_index >= SHARD - live - part * PART, found, -jnp.inf)
        return found

    def both(behind, ahead):
        high, parts = None, []
        if behind is not None:
            step, tile, kind = behind
            limit = best[tile]
            if kind != "home":
                before = top[tile]
                limit = jnp.maximum(before, limit)
        for part in range(SHARD // PART):
            rows = pl.ds(part * PART, PART)
            if ahead is not None:
                found = scored(*ahead, part)
                peak = jnp.max(found.reshape(PART // 8, 8, QB), axis=0)
                high = peak if high is None else jnp.maximum(high, peak)
            if behind is not None:
                parts.append(jnp.exp2(score[tile, rows, :] - limit).astype(bf16))
            if ahead is not None:
                score[ahead[1], rows, :] = found
        if behind is not None:
            summed = jnp.dot(
                vals[step], jnp.concatenate(parts, axis=0), preferred_element_type=f32
            )
            top[tile] = limit
            if kind == "home":
                acc[tile] = summed
            else:
                acc[tile] = acc[tile] * jnp.exp2(before - limit) + summed
        if ahead is not None:
            best[ahead[1]] = jnp.max(high, axis=0, keepdims=True)

    order = [(0, tile, "home") for tile in range(NQB)]
    order += [(length - 1, tile, "oldest") for tile in range(NQB)]
    count = len(order)
    order += [(1, tile, "whole") for tile in range(AHEAD)]
    for at in range(-AHEAD, count):
        both(order[at] if at >= 0 else None, order[at + AHEAD])

    def inner(step, carry):
        after = jnp.minimum(step + 1, length - 2)
        for tile in range(NQB):
            later = (tile + AHEAD) % NQB
            target = after if tile + AHEAD >= NQB else step
            both((step, tile, "whole"), (target, later, "whole"))
        return carry

    lax.fori_loop(1, length - 1, inner, 0)

    def finish(tile, carry):
        done = acc[tile, :DH] / acc[tile, DH : DH + 1]
        out[0, pl.ds(pl.multiple_of(tile * QB, QB), QB), :] = done.T.astype(bf16)
        return carry

    lax.fori_loop(0, NQB, finish, 0)


def attend(head, info, q_mine, q_theirs, turn, place, blocks):
    whole = pl.BlockSpec((2, 2, 3, DH, DH), lambda r, c: (0, 0, 0, 0, 0))
    q_spec = pl.BlockSpec((1, ROWS, DH), lambda r, c: (head, 0, 0))
    return pl.pallas_call(
        attend_kernel,
        out_shape=jax.ShapeDtypeStruct((2, ROWS, DH), bf16),
        grid_spec=pltpu.PrefetchScalarGridSpec(
            num_scalar_prefetch=1,
            grid=(2,),
            in_specs=[
                q_spec,
                q_spec,
                pl.BlockSpec(
                    (1, 1, CHAIN, 2 * DH, DH), lambda r, c: (r, place, 0, 0, 0)
                ),
            ]
            + [whole] * NEIGH,
            out_specs=pl.BlockSpec((1, ROWS, DH), lambda r, c: (r, 0, 0)),
            scratch_shapes=[
                pltpu.VMEM((CHAIN, SHARD, DH), bf16),
                pltpu.VMEM((CHAIN, DH + 16, SHARD), bf16),
                pltpu.VMEM((DH, ROWS), bf16),
                pltpu.VMEM((NQB, 1, QB), f32),
                pltpu.VMEM((NQB, 1, QB), f32),
                pltpu.VMEM((NQB, SHARD, QB), f32),
                pltpu.VMEM((NQB, DH + 16, QB), f32),
            ],
        ),
    )(info, q_mine, q_theirs, turn, *blocks)


def project_kernel(count, last, *refs):
    inputs = 4 * (2 * count + 2)
    atts = refs[: 8 * count]
    weights = refs[8 * count : inputs]
    rest = refs[inputs:]
    total = rest[0][...] if last else None
    for source in range(4):
        pair = [
            jnp.concatenate(
                [atts[2 * (source * count + h) + slot][0] for h in range(count)], axis=1
            )
            for slot in range(2)
        ]
        matrices = [
            weights[2 * source + slot][...].reshape(count * DH, -1) for slot in range(2)
        ]
        part = jnp.dot(
            jnp.concatenate(pair, axis=1),
            jnp.concatenate(matrices, axis=0),
            preferred_element_type=f32,
        )
        total = part if total is None else total + part
    rest[-1][...] = total.astype(rest[-1].dtype)


def project(atts, weights, first, total, dtype):
    count = len(atts[0])
    flat = [array for source in atts for both in source for array in both]
    flat_weights = [array for source in weights for array in source]
    att_specs = [
        pl.BlockSpec((1, BAND, DH), lambda r: (0, r, 0)),
        pl.BlockSpec((1, BAND, DH), lambda r: (1, r, 0)),
    ]
    weight_spec = pl.BlockSpec((count, DH, ROWS), lambda r: (first // count, 0, 0))
    total_spec = pl.BlockSpec((BAND, ROWS), lambda r: (r, 0))
    return pl.pallas_call(
        functools.partial(project_kernel, count, total is not None),
        out_shape=jax.ShapeDtypeStruct((ROWS, ROWS), dtype),
        grid=(ROWS // BAND,),
        in_specs=att_specs * (len(flat) // 2)
        + [weight_spec] * len(flat_weights)
        + ([total_spec] if total is not None else []),
        out_specs=total_spec,
    )(*flat, *flat_weights, *(() if total is None else (total,)))


def program(
    queries, cache_keys, cache_values, reflect, betas, chain_len, block_start, live_len, w_out
):
    here = lax.axis_index("ctx")
    group = lax.axis_index("head")
    core = here % 2
    z = (here % 8) // 2
    core_array = core[None].astype(jnp.int32)

    own_info = jnp.concatenate(
        [chain_len, live_len, block_start[0], jnp.zeros((2,), jnp.int32)]
    )
    info = jnp.concatenate([core_array, own_info, lax.ppermute(own_info, "ctx", SWAP)])

    kv_mine, kv_theirs, q_mine, q_theirs = pack(core_array, cache_keys, cache_values, queries)
    kv_other = lax.ppermute(kv_theirs, "ctx", SWAP)

    rates = jnp.pad(betas[0][:, None, :], ((0, 0), (0, 15), (0, DH - RANK)))
    factors = jnp.concatenate([reflect[0], rates], axis=1)
    factors_mine = lax.dynamic_slice_in_dim(factors, HALF * core, HALF, 0)
    factors_theirs = lax.dynamic_slice_in_dim(factors, HALF * (1 - core), HALF, 0)
    factors_pair = jnp.stack([factors_mine, lax.ppermute(factors_theirs, "ctx", SWAP)])
    factors_previous = lax.ppermute(factors_pair, "ctx", plane(1))
    factor_list = [factors_pair]
    for step in range(1, 4):
        chosen = jnp.where(z + step >= 4, factors_previous, factors_pair)
        factor_list.append(lax.ppermute(chosen, "ctx", along_z(step)))
    factor_list.append(factors_previous)
    q_other = lax.ppermute(q_theirs, "ctx", SWAP)

    pairs = [jnp.stack([kv_mine[h], kv_other[h]]) for h in range(HALF)]
    previous = [lax.ppermute(pairs[h], "ctx", plane(1)) for h in range(HALF)]
    blocks = []
    for h in range(HALF):
        picked = [
            jnp.where(z + step >= 4, previous[h], pairs[h]) for step in range(1, 4)
        ]
        arrived = [
            lax.ppermute(picked[step - 1], "ctx", along_z(step))
            for step in range(1, 4)
        ]
        blocks.append([pairs[h], *arrived, previous[h]])

    def columns_of(half, step):
        target = (group + step) % N_HEAD
        block = lax.dynamic_slice(
            w_out, (half * HALF * DH, target * ROWS), (HALF * DH, ROWS)
        )
        return block.reshape(HALF, DH, ROWS)

    weights = [(columns_of(core, 0), columns_of(1 - core, 0))]
    for step in range(1, N_HEAD):
        fetched = lax.ppermute(columns_of(core, step), "head", along_y(step))
        weights.append((fetched, lax.ppermute(fetched, "ctx", SWAP)))

    turn_first = turns(core_array, factor_list, 0, 1)
    turn_rest = turns(core_array, factor_list, 1, HALF - 1)
    atts = [[] for _ in range(N_HEAD)]
    for h in range(HALF):
        turn, place = (turn_rest, h - 1) if h else (turn_first, 0)
        rows = attend(h, info, q_mine, q_other, turn, place, blocks[h])
        late = h < HALF - 1
        if not late:
            rows = jnp.stack([rows[0], lax.ppermute(rows[1], "ctx", SWAP)])
        for step in range(N_HEAD):
            piece = rows
            if step:
                piece = lax.ppermute(rows, "head", along_y(step))
            other = lax.ppermute(piece, "ctx", SWAP) if late else piece
            atts[step].append((piece, other))
    total = project([a[:3] for a in atts], weights, 0, None, f32)
    return project([a[3:] for a in atts], weights, 3, total, bf16)


def solution(mesh):
    spec = P("ctx", "head")
    return jax.shard_map(
        program,
        mesh=mesh,
        in_specs=(
            spec,
            spec,
            spec,
            P("ctx", "head", None, None),
            P("ctx", "head", None),
            P("ctx"),
            P("ctx", None),
            P("ctx"),
            P("head", None),
        ),
        out_specs=spec,
        check_vma=False,
    )
```
